128 devices in a mesh: lon: 16 (over x, y_hi, core), lat: 8 (over y_lo, z).
Axes of the slice: x: 4, y: 4 (y_hi: 2, y_lo: 2; y = y_hi * 2 + y_lo), z: 4, core: 2. Of those that a mesh axis runs over, the one named last changes fastest.
Arguments:
- air_state: bfloat16 [4, 48, 384, 192], P(None, 'lat', 'lon'), may hold values from -6 to 6
- upstream: bfloat16 [4, 48, 384, 192], P(None, 'lat', 'lon'), may hold values from -6 to 6
- norm_gain: float32 [192], replicated, may hold values from 0.25 to 1.75
- w_qkv: bfloat16 [192, 576], replicated, may hold values from -0.4375 to 0.4375
- w_proj: bfloat16 [192, 192], replicated, may hold values from -0.4375 to 0.4375
- bias_table: float32 [8, 2, 6, 3312], P('lat'), may hold values from -5 to 260
Outputs:
- block_out: bfloat16 [4, 48, 384, 192], P(None, 'lat', 'lon')
- d_state: bfloat16 [4, 48, 384, 192], P(None, 'lat', 'lon')
- d_gain: float32 [192], replicated
- d_wqkv: float32 [192, 576], replicated
- d_wproj: float32 [192, 192], replicated
- d_table: float32 [8, 2, 6, 3312], P('lat')
The draws below stay inside these ranges and needn't reach their ends.
All inputs are finite; a program needn't handle non-finite values.
Results may differ from the reference program's by a relative error of at most 0.019.
Values may be sent and summed in bfloat16 or wider, within the bound.
No kernel may reach another device: no remote copies, remote signals or barrier semaphores. Data moves between devices by JAX's collectives and lax.ppermute only.
A program may use at most 128 MiB of HBM per device.

```python
from functools import partial
import jax
import jax.numpy as jnp
from jax import lax

C = 192
HEADS = 6
WLEV = 2
WLAT = 6
WLON = 12
LEV = 4
WIN = 144
REL = 3312
LEVW = 2
LAT = 48
LON = 384
BANDS = 8


def draw_bias_table(key, part):
    base_key = jax.random.fold_in(key, 11)
    shape = (BANDS, LEVW, HEADS, REL)
    return jnp.clip(jax.random.normal(base_key, shape, jnp.float32), -5.0, 5.0)


def level_of(own_key, shape, pieces, least, largest):
    factor_of, own = 1.0, jax.random.fold_in(own_key, 6)
    for axis_at, parts in pieces:
        steps = jnp.exp(jax.random.uniform(jax.random.fold_in(own, axis_at), (parts,), jnp.float32, least / len(pieces), largest / len(pieces)))
        factor_of = factor_of * jnp.repeat(steps, shape[axis_at] // parts).reshape([-1 if axis == axis_at else 1 for axis in range(len(shape))])
    return factor_of


def bell_draw(key, extent, spread, most, pieces=(), held_as=jnp.bfloat16):
    entries = jax.random.normal(key, extent, jnp.float32) * spread
    if len(pieces) > 0:
        entries = level_of(key, extent, pieces, -0.22, 0.18) * entries
    return jnp.clip(entries, min=-most, max=most).astype(held_as)


def setup_inputs(seed: int = 0) -> dict:
    key_of = jax.random.split(jax.random.key(seed), 7)
    return {
        "air_state": bell_draw(key_of[0], (LEV, LAT, LON, C), 1.0, 6.0, ((1, 8), (2, 16))),
        "upstream": bell_draw(key_of[1], (LEV, LAT, LON, C), 1.0, 6.0, ((1, 8), (2, 16))),
        "norm_gain": jnp.clip(1.0 + 0.15 * jax.random.normal(key_of[2], (C,), jnp.float32), 0.25, 1.75),
        "w_qkv": bell_draw(key_of[3], (C, 3 * C), C ** -0.5, 0.4375),
        "w_proj": bell_draw(key_of[4], (C, C), C ** -0.5, 0.4375),
        "bias_table": draw_bias_table(jax.random.fold_in(key_of[6], 71), 0),
    }


epsilon = 1e-05
masked_score = -1000000000.0

def layer_norm(as_input, gain_vec):
    average = lax.optimization_barrier(jnp.mean(as_input, axis=-1, keepdims=True))
    centred = as_input - average
    variance = lax.optimization_barrier(jnp.mean(centred * centred, axis=-1, keepdims=True))
    return centred * lax.rsqrt(variance + epsilon) * gain_vec

def attention_core(qkv_rows, table_row, first_row, lat_total):
    lev_count, col_count = (qkv_rows.shape[0], qkv_rows.shape[2])
    head_width = qkv_rows.shape[5]
    lev_wins, lon_wins = (lev_count // WLEV, col_count // WLON)
    windowed = qkv_rows.reshape(lev_wins, WLEV, WLAT, lon_wins, WLON, 3, HEADS, head_width)
    windowed = windowed.transpose(5, 0, 3, 6, 1, 2, 4, 7).reshape(3, lev_wins, lon_wins, HEADS, WIN, head_width)
    queries, keyset, values = (windowed[0], windowed[1], windowed[2])
    scores = jnp.einsum('achid,achjd->achij', queries, keyset, preferred_element_type=jnp.float32) * head_width ** (-0.5)
    picked = table_row.reshape(lev_wins, HEADS, WLEV * WLAT, WLEV * WLAT, 2 * WLON - 1)
    offsets = jnp.arange(WLON)
    onehot = (offsets[None, :, None] - offsets[:, None, None] + WLON - 1 == jnp.arange(2 * WLON - 1)[None, None, :]).astype(jnp.float32)
    expanded = jnp.einsum('ahpqr,ijr->ahpiqj', picked, onehot, precision=lax.Precision.HIGHEST)
    expanded = expanded.reshape(lev_wins, 1, HEADS, WIN, WIN)
    scores = scores + expanded
    lev_index = jnp.arange(lev_wins * WLEV).reshape(lev_wins, WLEV)
    lev_part = (lev_index >= lev_count - WLEV // 2).astype(jnp.int32)
    lat_index = first_row + jnp.arange(WLAT, dtype=jnp.int32)
    lat_part = (lat_index >= lat_total - WLAT // 2).astype(jnp.int32)
    region = 2 * lev_part[:, :, None, None] + lat_part[None, None, :, None] + jnp.zeros((1, 1, 1, WLON), jnp.int32)
    region = region.reshape(lev_wins, WIN)
    same_region = region[:, None, None, :, None] == region[:, None, None, None, :]
    scores = jnp.where(same_region, scores, masked_score)
    row_max = lax.stop_gradient(lax.optimization_barrier(jnp.max(scores, axis=-1, keepdims=True)))
    weights = jnp.exp(scores - row_max)
    softened = (weights / lax.optimization_barrier(jnp.sum(weights, axis=-1, keepdims=True))).astype(jnp.bfloat16)
    mixture = jnp.einsum('achij,achjd->achid', softened, values, preferred_element_type=jnp.float32).astype(jnp.bfloat16)
    mixture = mixture.reshape(lev_wins, lon_wins, HEADS, WLEV, WLAT, WLON, head_width)
    return mixture.transpose(0, 3, 4, 1, 5, 2, 6).reshape(lev_count, WLAT, col_count, HEADS * head_width)

def local_sublayer(shifted, shifted_up, gain_vec, w_qkv, w_proj, table_row, first_row, lat_total):
    lev_count, row_count, col_count, width = shifted.shape
    pre_norm, norm_back = jax.vjp(layer_norm, shifted.astype(jnp.float32), gain_vec)
    normed = pre_norm.astype(jnp.bfloat16).reshape(-1, width)
    qkv_rows = jnp.dot(normed, w_qkv, preferred_element_type=jnp.float32).astype(jnp.bfloat16)
    qkv_rows = qkv_rows.reshape(lev_count, row_count, col_count, 3, HEADS, width // HEADS)
    core_fn = partial(attention_core, first_row=first_row, lat_total=lat_total)
    mixture, core_back = jax.vjp(core_fn, qkv_rows, table_row)
    flat_rows = mixture.reshape(-1, width)
    branch = jnp.dot(flat_rows, w_proj, preferred_element_type=jnp.float32).astype(jnp.bfloat16)
    up_rows = shifted_up.reshape(-1, width)
    d_proj = jnp.einsum('ti,to->io', flat_rows, up_rows, preferred_element_type=jnp.float32)
    d_mixed = jnp.einsum('to,io->ti', up_rows, w_proj, preferred_element_type=jnp.float32).astype(jnp.bfloat16)
    d_qkv, d_row = core_back(d_mixed.reshape(mixture.shape))
    d_qkv = d_qkv.reshape(-1, 3 * width)
    d_wqkv = jnp.einsum('ti,to->io', normed, d_qkv, preferred_element_type=jnp.float32)
    d_normed = jnp.einsum('to,io->ti', d_qkv, w_qkv, preferred_element_type=jnp.float32)
    d_input, d_gain = norm_back(d_normed.reshape(lev_count, row_count, col_count, width))
    branch = branch.reshape(lev_count, row_count, col_count, width)
    return (branch, d_input.astype(jnp.bfloat16), d_gain, d_wqkv, d_proj, d_row)

def reference(air_state, upstream, norm_gain, w_qkv, w_proj, bias_table):
    lev_shift, lat_shift, lon_shift = (WLEV // 2, WLAT // 2, WLON // 2)
    rolled = jnp.roll(air_state, (-lev_shift, -lat_shift, -lon_shift), (0, 1, 2))
    rolled_up = jnp.roll(upstream, (-lev_shift, -lat_shift, -lon_shift), (0, 1, 2))
    lat_total = air_state.shape[1]
    width = air_state.shape[3]

    def row_step(totals, window_row):
        first_row = window_row * WLAT
        block_in = lax.dynamic_slice_in_dim(rolled, first_row, WLAT, 1)
        block_up = lax.dynamic_slice_in_dim(rolled_up, first_row, WLAT, 1)
        table_row = lax.dynamic_index_in_dim(bias_table, window_row, 0, keepdims=False)
        results = local_sublayer(block_in, block_up, norm_gain, w_qkv, w_proj, table_row, first_row, lat_total)
        totals = tuple((before + added for before, added in zip(totals, results[2:5])))
        return (totals, (results[0], results[1], results[5]))
    zeros_init = (jnp.zeros((width,), jnp.float32), jnp.zeros((width, 3 * width), jnp.float32), jnp.zeros((width, width), jnp.float32))
    totals, (branches, gradients, d_table) = lax.scan(row_step, zeros_init, jnp.arange(lat_total // WLAT, dtype=jnp.int32))
    shape_out = air_state.shape
    branches = branches.transpose(1, 0, 2, 3, 4).reshape(shape_out)
    gradients = gradients.transpose(1, 0, 2, 3, 4).reshape(shape_out)
    branches = jnp.roll(branches, (lev_shift, lat_shift, lon_shift), (0, 1, 2))
    gradients = jnp.roll(gradients, (lev_shift, lat_shift, lon_shift), (0, 1, 2))
    block_out = (air_state.astype(jnp.float32) + branches.astype(jnp.float32)).astype(jnp.bfloat16)
    d_state = (upstream.astype(jnp.float32) + gradients.astype(jnp.float32)).astype(jnp.bfloat16)
    return (block_out, d_state, totals[0], totals[1], totals[2], d_table)
```

```python
import functools

import jax
import jax.numpy as jnp
from jax import lax
from jax.experimental import pallas as pl
from jax.experimental.pallas import tpu as pltpu
from jax.sharding import PartitionSpec as P

HEADS = 6
HEAD = 32
WLEV = 2
WLAT = 6
WLON = 12
WIN = 144
POS = WLEV * WLAT
REL = 2 * WLON - 1
C = 192
TOK = 576
WROWS = 80
TROWS = 32
CHUNK = WROWS + TROWS

epsilon = 1e-05
masked_score = -1000000000.0
f32 = jnp.float32
bf16 = jnp.bfloat16

NN = (((1,), (0,)), ((), ()))
NT = (((1,), (1,)), ((), ()))
TN = (((0,), (0,)), ((), ()))


def dot(a, b, dims):
    return lax.dot_general(a, b, dims, preferred_element_type=f32)


def window_parts():
    for a in range(2):
        for s in range(WLEV):
            for lat in range(WLAT):
                p = s * WLAT + lat
                yield (2 * a + s + 1) % 4, lat, a * 2 * WIN + p, (a * 2 + 1) * WIN + p


def put(dst, start, rows):
    n = rows.shape[0]
    dst[pl.ds(start, n, stride=POS), :] = rows[:, :128]
    high = jnp.concatenate([rows[:, 128:], jnp.zeros((n, 64), f32)], axis=1)
    dst[pl.ds(TOK + start, n, stride=POS), :] = high


def get(src, start):
    low = src[pl.ds(start, WLON, stride=POS), :]
    high = src[pl.ds(TOK + start, WLON, stride=POS), :]
    return jnp.concatenate([low, high[:, :64]], axis=1).astype(bf16)


def whole_rows(src):
    return jnp.concatenate([src[:TOK], src[TOK:][:, :64]], axis=1)


def hold(dst, rows):
    dst[:TOK] = rows[:, :128]
    dst[TOK:, :64] = rows[:, 128:]


def main_kernel(
    last_ref, air_ref, up_ref, lonh_ref, lath_ref, corh_ref, gain_ref, wqkv_ref, wproj_ref, tab_ref,
    own_ref, lono_ref, lato_ref, coro_ref, grad_ref,
    xt, ut, bias, dbias, q_s, k_s, v_s, dm_s, mix_s, dq_s, dk_s, dv_s, gw, gt,
):
    for i, (src, dst) in enumerate(((air_ref, xt), (up_ref, ut))):
        for lev, lat, w0, w1 in window_parts():
            if lat < 3:
                row = src[lev, lat + 3].astype(f32)
                first, second = row[6:18], row[18:24]
                third = lonh_ref[i, lev, lat].astype(f32)
            else:
                row = lath_ref[i, lev, lat - 3].astype(f32)
                first, second = row[0:12], row[12:18]
                third = corh_ref[i, lev, lat - 3].astype(f32)
            put(dst, w0, first)
            put(dst, w1, second)
            put(dst, w1 + 72, third)

    for a in range(2):
        for h in range(HEADS):
            rows = pl.ds((a * HEADS + h) * POS, POS)
            for lon in range(WLON):
                bias[a, lon * POS : (lon + 1) * POS, h * WIN : (h + 1) * WIN] = tab_ref[
                    rows, (11 - lon) * POS : (11 - lon) * POS + WIN
                ]
    is_last = last_ref[0]
    for a in range(2):
        pj = lax.broadcasted_iota(jnp.int32, (WIN, 1), 0) % POS
        pi = lax.broadcasted_iota(jnp.int32, (1, HEADS * WIN), 1) % POS

        def region(p):
            lev_part = jnp.where(p >= WLAT, 2 * a, 0)
            lat_part = jnp.where((p % WLAT) >= WLAT // 2, is_last, 0)
            return lev_part + lat_part

        bias[a] = jnp.where(region(pj) == region(pi), bias[a], masked_score)
    dbias[...] = jnp.zeros_like(dbias)

    x = whole_rows(xt)
    mean = jnp.sum(x, axis=1, keepdims=True) * (1.0 / C)
    centred = x - mean
    var = jnp.sum(centred * centred, axis=1, keepdims=True) * (1.0 / C)
    rstd = lax.rsqrt(var + epsilon)
    gain = gain_ref[...]
    normed = (centred * rstd * gain).astype(bf16)
    for part, dst in enumerate((q_s, k_s, v_s)):
        dst[...] = dot(normed, wqkv_ref[:, part * C : (part + 1) * C], NN).astype(bf16)
    up = whole_rows(ut).astype(bf16)
    dm_s[...] = dot(up, wproj_ref[...], NT).astype(bf16)

    scale = HEAD**-0.5
    lane_head = lax.broadcasted_iota(jnp.int32, (1, C), 1) // HEAD

    def spread(rows):
        zero = jnp.zeros_like(rows)
        return jnp.concatenate([jnp.where(lane_head == h, rows, zero) for h in range(HEADS)], axis=0)

    def gathered(stacked):
        total = stacked[0:WIN]
        for h in range(1, HEADS):
            total = jnp.where(lane_head == h, stacked[h * WIN : (h + 1) * WIN], total)
        return total

    def window(w, carry):
        a = w // 2
        rows = pl.ds(pl.multiple_of(w * WIN, 16), WIN)
        k, v = k_s[rows, :], v_s[rows, :]
        qs = spread(q_s[rows, :])
        scores = dot(k, qs, NT) * scale + bias[a]
        top = jnp.max(scores, axis=0, keepdims=True)
        weights = jnp.exp(scores - top)
        probs = weights * (1.0 / jnp.sum(weights, axis=0, keepdims=True))
        soft = probs.astype(bf16)
        mix_s[rows, :] = gathered(dot(soft, v, TN)).astype(bf16)
        ds = spread(dm_s[rows, :])
        dprobs = dot(v, ds, NT)
        dv_s[rows, :] = dot(soft, ds, NN).astype(bf16)
        inner = jnp.sum(probs * dprobs, axis=0, keepdims=True)
        dscores = probs * (dprobs - inner)
        dbias[a] += dscores
        dsc = dscores.astype(bf16)
        dk_s[rows, :] = (dot(dsc, qs, NN) * scale).astype(bf16)
        dq_s[rows, :] = (gathered(dot(dsc, k, TN)) * scale).astype(bf16)
        return carry

    lax.fori_loop(0, 4, window, 0)

    mix = mix_s[...]
    dq, dk, dv = dq_s[...], dk_s[...], dv_s[...]
    mats = [dot(normed, d, TN) for d in (dq, dk, dv)] + [dot(mix, up, TN)]
    for t, m in enumerate(mats):
        gw[t * C : (t + 1) * C, :] = m[:, 0:128].astype(bf16)
    for t in range(2):
        both = jnp.concatenate([mats[2 * t][:, 128:192], mats[2 * t + 1][:, 128:192]], axis=1)
        gw[(4 + t) * C : (5 + t) * C, :] = both.astype(bf16)

    branch = dot(mix, wproj_ref[...], NN).astype(bf16).astype(f32)
    dnorm = (
        dot(dq, wqkv_ref[:, 0:C], NT)
        + dot(dk, wqkv_ref[:, C : 2 * C], NT)
        + dot(dv, wqkv_ref[:, 2 * C : 3 * C], NT)
    )
    xhat = centred * rstd
    dgain = jnp.sum(dnorm * xhat, axis=0, keepdims=True)
    dhat = dnorm * gain
    m1 = jnp.sum(dhat, axis=1, keepdims=True) * (1.0 / C)
    m2 = jnp.sum(dhat * xhat, axis=1, keepdims=True) * (1.0 / C)
    dx = rstd * (dhat - m1 - xhat * m2)
    gw[6 * C :, :] = jnp.zeros((16 * WROWS - 6 * C, 128), bf16)
    row_of = lax.broadcasted_iota(jnp.int32, (16, 128), 0)
    dg0 = dgain[:, 0:128]
    dg1 = jnp.concatenate([dgain[:, 128:192], jnp.zeros((1, 64), f32)], axis=1)
    gw[6 * C : 6 * C + 16, :] = jnp.where(
        row_of == 0, dg0, jnp.where(row_of == 1, dg1, jnp.zeros((16, 128), f32))
    ).astype(bf16)

    hold(xt, branch)
    hold(ut, dx)
    for i, src in enumerate((xt, ut)):
        for lev, lat, w0, w1 in window_parts():
            first = get(src, w0)
            rest = get(src, w1)
            if lat < 3:
                own_ref[i, lev, lat, 0:12] = first
                own_ref[i, lev, lat, 12:18] = rest[0:6]
                lono_ref[i, lev, lat] = rest[6:12]
            else:
                lato_ref[i, lev, lat - 3, 0:12] = first
                lato_ref[i, lev, lat - 3, 12:18] = rest[0:6]
                coro_ref[i, lev, lat - 3] = rest[6:12]

    gt[...] = jnp.zeros_like(gt)
    for a in range(2):
        for h in range(HEADS):
            rows = pl.ds((a * HEADS + h) * POS, POS)
            for lon in range(WLON):
                gt[rows, (11 - lon) * POS : (11 - lon) * POS + WIN] += dbias[
                    a, lon * POS : (lon + 1) * POS, h * WIN : (h + 1) * WIN
                ]
    gtb = gt[...].astype(bf16)
    table_rows = jnp.concatenate(
        [gtb[:, 0:128], gtb[:, 128:256], gtb[:, 256:384], jnp.zeros((80, 128), bf16)], axis=0
    )
    for i in range(16):
        grad_ref[i, 0:WROWS] = gw[i * WROWS : (i + 1) * WROWS, :]
        grad_ref[i, WROWS:CHUNK] = table_rows[i * TROWS : (i + 1) * TROWS]


def run_main(last, air, up, lonh, lath, corh, gain, wqkv, wproj, tab):
    vmem = pl.BlockSpec(memory_space=pltpu.VMEM)
    smem = pl.BlockSpec(memory_space=pltpu.SMEM)
    tok = lambda dt: pltpu.VMEM((TOK, C), dt)
    return pl.pallas_call(
        main_kernel,
        in_specs=[smem] + [vmem] * 9,
        out_specs=[vmem] * 5,
        out_shape=[
            jax.ShapeDtypeStruct((2, 4, 3, 18, C), bf16),
            jax.ShapeDtypeStruct((2, 4, 3, 6, C), bf16),
            jax.ShapeDtypeStruct((2, 4, 3, 18, C), bf16),
            jax.ShapeDtypeStruct((2, 4, 3, 6, C), bf16),
            jax.ShapeDtypeStruct((16, CHUNK, 128), bf16),
        ],
        scratch_shapes=[
            pltpu.VMEM((2 * TOK, 128), f32),
            pltpu.VMEM((2 * TOK, 128), f32),
            pltpu.VMEM((2, WIN, HEADS * WIN), f32),
            pltpu.VMEM((2, WIN, HEADS * WIN), f32),
        ]
        + [tok(bf16)] * 8
        + [pltpu.VMEM((16 * WROWS, 128), bf16), pltpu.VMEM((WIN, 384), f32)],
        compiler_params=pltpu.CompilerParams(vmem_limit_bytes=48 << 20),
        name="sublayer",
    )(last, air, up, lonh, lath, corh, gain, wqkv, wproj, tab)


def neighbour(array, lon_by, lat_by):
    lons, lats = lax.axis_size("lon"), lax.axis_size("lat")
    if lat_by == 0:
        return lax.ppermute(array, "lon", [(i, (i + lon_by) % lons) for i in range(lons)])
    if lon_by == 0:
        return lax.ppermute(array, "lat", [(i, (i + lat_by) % lats) for i in range(lats)])
    pairs = [
        (i * lats + j, ((i + lon_by) % lons) * lats + (j + lat_by) % lats)
        for i in range(lons)
        for j in range(lats)
    ]
    return lax.ppermute(array, ("lon", "lat"), pairs)


def each(array, axis):
    copies = jnp.broadcast_to(array, (lax.axis_size(axis), *array.shape))
    return lax.all_to_all(copies, axis, split_axis=0, concat_axis=0, tiled=True)


def summed(array):
    return jnp.sum(array.astype(f32), axis=0).astype(bf16)


def on_device(air, up, gain, wqkv, wproj, table):
    both = jnp.stack([air, up])
    lonh = neighbour(both[:, :, 3:6, 0:6], -1, 0)
    lath = neighbour(both[:, :, 0:3, 6:24], 0, -1)
    corh = neighbour(both[:, :, 0:3, 0:6], -1, -1)
    last = (lax.axis_index("lat") == lax.axis_size("lat") - 1).astype(jnp.int32).reshape(1)
    tab = table.reshape(12, POS, POS, REL)[:, :, :, ::-1].transpose(0, 2, 3, 1)
    tab = tab.reshape(12 * POS, REL * POS)
    own, lono, lato, coro, grads = run_main(
        last, air, up, lonh, lath, corh, gain.reshape(1, C), wqkv, wproj, tab
    )
    lonr = neighbour(lono, 1, 0)
    latr = neighbour(lato, 0, 1)
    corr = neighbour(coro, 1, 1)

    part = summed(lax.all_to_all(grads, "lon", split_axis=0, concat_axis=0, tiled=True))
    weights = summed(each(part[:WROWS], "lat"))
    whole = each(jnp.concatenate([weights, part[WROWS:]], axis=0), "lon")

    top = jnp.concatenate([corr, latr], axis=3)
    low = jnp.concatenate([lonr, own], axis=3)
    add = jnp.concatenate([top, low], axis=2).astype(f32)
    block_out = (air.astype(f32) + add[0]).astype(bf16)
    d_state = (up.astype(f32) + add[1]).astype(bf16)

    gw = whole[:, :WROWS].reshape(16 * WROWS, 128).astype(f32)
    tiles = [gw[t * C : (t + 1) * C] for t in range(6)]
    dwq = jnp.concatenate([tiles[0], tiles[4][:, :64]], axis=1)
    dwk = jnp.concatenate([tiles[1], tiles[4][:, 64:]], axis=1)
    dwv = jnp.concatenate([tiles[2], tiles[5][:, :64]], axis=1)
    d_wproj = jnp.concatenate([tiles[3], tiles[5][:, 64:]], axis=1)
    d_wqkv = jnp.concatenate([dwq, dwk, dwv], axis=1)
    d_gain = jnp.concatenate([gw[6 * C], gw[6 * C + 1, :64]])
    gt = whole[:, WROWS:].reshape(16 * TROWS, 128)[: 3 * WIN].reshape(3, WIN, 128)
    gt = gt.transpose(1, 0, 2).reshape(WIN, 384)[:, : REL * POS].astype(f32)
    gt = gt.reshape(12, POS, REL, POS).transpose(0, 3, 1, 2)[:, :, :, ::-1]
    d_table = gt.reshape(1, 2, HEADS, POS * POS * REL)
    return (block_out, d_state, d_gain, d_wqkv, d_wproj, d_table)


def solution(mesh):
    grid = P(None, "lat", "lon", None)
    return jax.shard_map(
        on_device,
        mesh=mesh,
        in_specs=(grid, grid, P(), P(), P(), P("lat", None, None, None)),
        out_specs=(grid, grid, P(), P(), P(), P("lat", None, None, None)),
        check_vma=False,
    )
```

```python
import functools

import jax
import jax.numpy as jnp
from jax import lax
from jax.experimental import pallas as pl
from jax.experimental.pallas import tpu as pltpu
from jax.sharding import PartitionSpec as P

HEADS = 6
HEAD = 32
WLEV = 2
WLAT = 6
WLON = 12
WIN = 144
POS = WLEV * WLAT
REL = 2 * WLON - 1
C = 192
TOK = 576
SHARES = 16
WROWS = 72
GROW = 72
TROW = 76
TROWS = 20
CHUNK = 96
MID = 80
LANES = REL * POS

epsilon = 1e-05
masked_score = -1000000000.0
f32 = jnp.float32
bf16 = jnp.bfloat16

NN = (((1,), (0,)), ((), ()))
NT = (((1,), (1,)), ((), ()))
TN = (((0,), (0,)), ((), ()))


def dot(a, b, dims):
    return lax.dot_general(a, b, dims, preferred_element_type=f32)


def window_parts():
    for a in range(2):
        for s in range(WLEV):
            for lat in range(WLAT):
                p = s * WLAT + lat
                yield (2 * a + s + 1) % 4, lat, a * 2 * WIN + p, (a * 2 + 1) * WIN + p


def put(dst, start, rows):
    n = rows.shape[0]
    dst[pl.ds(start, n, stride=POS), :] = rows[:, :128]
    high = jnp.concatenate([rows[:, 128:], jnp.zeros((n, 64), f32)], axis=1)
    dst[pl.ds(TOK + start, n, stride=POS), :] = high


def get(src, start):
    low = src[pl.ds(start, WLON, stride=POS), :]
    high = src[pl.ds(TOK + start, WLON, stride=POS), :]
    return jnp.concatenate([low, high[:, :64]], axis=1)


def whole_rows(src):
    return jnp.concatenate([src[:TOK], src[TOK:][:, :64]], axis=1)


def hold(dst, rows):
    dst[:TOK] = rows[:, :128]
    dst[TOK:, :64] = rows[:, 128:]


def joined(state, up):
    return jnp.concatenate([state[:, :128], up[:, :128], state[:, 128:], up[:, 128:]], axis=1)


def parted(rows):
    state = jnp.concatenate([rows[:, 0:128], rows[:, 256:320]], axis=1)
    return state, jnp.concatenate([rows[:, 128:256], rows[:, 320:384]], axis=1)


def pack_kernel(air_ref, up_ref, lonh_ref, lath_ref, corh_ref):
    for lev in range(4):
        for r in range(3):
            at = lev * 3 + r
            row = joined(air_ref[lev, r].astype(f32), up_ref[lev, r].astype(f32)).astype(bf16)
            corh_ref[at * 6 : (at + 1) * 6] = row[0:6]
            lath_ref[at * 18 : (at + 1) * 18] = row[6:24]
            row = joined(
                air_ref[lev, r + 3][0:6].astype(f32), up_ref[lev, r + 3][0:6].astype(f32)
            )
            lonh_ref[at * 6 : (at + 1) * 6] = row.astype(bf16)


HALOS = [
    jax.ShapeDtypeStruct((72, 2 * C), bf16),
    jax.ShapeDtypeStruct((216, 2 * C), bf16),
    jax.ShapeDtypeStruct((72, 2 * C), bf16),
]


def pack(air, up):
    vmem = pl.BlockSpec(memory_space=pltpu.VMEM)
    return pl.pallas_call(
        pack_kernel,
        in_specs=[vmem] * 2,
        out_specs=[vmem] * 3,
        out_shape=HALOS,
        name="pack",
    )(air, up)


def normalised(x):
    mean = jnp.sum(x, axis=1, keepdims=True) * (1.0 / C)
    centred = x - mean
    var = jnp.sum(centred * centred, axis=1, keepdims=True) * (1.0 / C)
    rstd = lax.rsqrt(var + epsilon)
    return centred * rstd, rstd


def onehots():
    src = lax.broadcasted_iota(jnp.int32, (384, 384), 0)
    dst = lax.broadcasted_iota(jnp.int32, (384, 384), 1)
    wanted = (dst % POS) * REL + (REL - 1 - dst // POS)
    lanes = ((src == wanted) & (dst < LANES)).astype(f32).astype(bf16)
    to = lax.broadcasted_iota(jnp.int32, (WIN, 192), 0)
    at = lax.broadcasted_iota(jnp.int32, (WIN, 192), 1)
    ah = to // POS
    rows = (at == (to % POS) * 16 + (ah % HEADS) * 2 + ah // HEADS).astype(f32).astype(bf16)
    return lanes, rows


def prep_kernel(last_ref, table_ref, bias, apart, held):
    entries = jnp.concatenate([table_ref[h] for h in range(HEADS)], axis=0)
    apart[...] = jnp.zeros_like(apart)
    for pj in range(POS):
        for pi in range(POS):
            at = (pi * POS + pj) * REL
            apart[pj * 16 : pj * 16 + POS, pi * REL : (pi + 1) * REL] = entries[:, at : at + REL]
    lanes, rows = onehots()
    left = apart[...]
    total = None
    for _ in range(3):
        piece = left.astype(bf16)
        left = left - piece.astype(f32)
        moved = dot(rows, dot(piece, lanes, NN).astype(bf16), NN)
        total = moved if total is None else total + moved
    held[...] = total
    for a in range(2):
        for h in range(HEADS):
            at = (a * HEADS + h) * POS
            for lon in range(WLON):
                bias[a, lon * POS : (lon + 1) * POS, h * WIN : (h + 1) * WIN] = held[
                    at : at + POS, (11 - lon) * POS : (11 - lon) * POS + WIN
                ]
    is_last = last_ref[0]
    for a in range(2):
        pj = lax.broadcasted_iota(jnp.int32, (WIN, 1), 0) % POS
        pi = lax.broadcasted_iota(jnp.int32, (1, HEADS * WIN), 1) % POS

        def region(p):
            lev_part = jnp.where(p >= WLAT, 2 * a, 0)
            lat_part = jnp.where((p % WLAT) >= WLAT // 2, is_last, 0)
            return lev_part + lat_part

        bias[a] = jnp.where(region(pj) == region(pi), bias[a], masked_score)


def prep(last, table):
    vmem = pl.BlockSpec(memory_space=pltpu.VMEM)
    smem = pl.BlockSpec(memory_space=pltpu.SMEM)
    return pl.pallas_call(
        prep_kernel,
        in_specs=[smem, vmem],
        out_specs=vmem,
        out_shape=jax.ShapeDtypeStruct((2, WIN, HEADS * WIN), f32),
        scratch_shapes=[pltpu.VMEM((192, 384), f32), pltpu.VMEM((WIN, 384), f32)],
        compiler_params=pltpu.CompilerParams(vmem_limit_bytes=16 << 20),
        cost_estimate=pl.CostEstimate(flops=10**8, bytes_accessed=2 << 20, transcendentals=0),
        name="prep",
    )(last, table)


def main_kernel(
    air_ref, up_ref, lonh_ref, lath_ref, corh_ref, gain_ref, wqkv_ref, wproj_ref, bias,
    own_ref, lono_ref, lato_ref, coro_ref, grad_ref,
    xt, ut, dbias, q_s, k_s, v_s, dm_s, mix_s, dq_s, dk_s, dv_s, gw, gt, tr, one,
):
    for lev, lat, w0, w1 in window_parts():
        at = lev * 3 + lat % 3
        if lat < 3:
            rows = [src[lev, lat + 3].astype(f32) for src in (air_ref, up_ref)]
            far = parted(lonh_ref[at * 6 : (at + 1) * 6].astype(f32))
            shift = 6
        else:
            rows = parted(lath_ref[at * 18 : (at + 1) * 18].astype(f32))
            far = parted(corh_ref[at * 6 : (at + 1) * 6].astype(f32))
            shift = 0
        for dst, row, edge in zip((xt, ut), rows, far):
            put(dst, w0, row[shift : shift + 12])
            put(dst, w1, row[shift + 12 : shift + 18])
            put(dst, w1 + 72, edge)

    dbias[...] = jnp.zeros_like(dbias)

    x = whole_rows(xt)
    xhat, rstd = normalised(x)
    normed = (xhat * gain_ref[...]).astype(bf16)
    for part, dst in enumerate((q_s, k_s, v_s)):
        dst[...] = dot(normed, wqkv_ref[:, part * C : (part + 1) * C], NN).astype(bf16)
    up = whole_rows(ut).astype(bf16)
    dm_s[...] = dot(up, wproj_ref[...], NT).astype(bf16)

    scale = HEAD**-0.5
    lane_head = lax.broadcasted_iota(jnp.int32, (1, C), 1) // HEAD

    def spread(rows):
        zero = jnp.zeros_like(rows)
        return jnp.concatenate([jnp.where(lane_head == h, rows, zero) for h in range(HEADS)], axis=0)

    def gathered(stacked):
        total = stacked[0:WIN]
        for h in range(1, HEADS):
            total = jnp.where(lane_head == h, stacked[h * WIN : (h + 1) * WIN], total)
        return total

    def window(w, carry):
        a = w // 2
        rows = pl.ds(pl.multiple_of(w * WIN, 16), WIN)
        k, v = k_s[rows, :], v_s[rows, :]
        qs = spread(q_s[rows, :])
        scores = dot(k, qs, NT) * scale + bias[a]
        top = jnp.max(scores, axis=0, keepdims=True)
        weights = jnp.exp(scores - top)
        probs = weights * (1.0 / jnp.sum(weights, axis=0, keepdims=True))
        soft = probs.astype(bf16)
        mix_s[rows, :] = gathered(dot(soft, v, TN)).astype(bf16)
        ds = spread(dm_s[rows, :])
        dprobs = dot(v, ds, NT)
        dv_s[rows, :] = dot(soft, ds, NN).astype(bf16)
        inner = jnp.sum(probs * dprobs, axis=0, keepdims=True)
        dscores = probs * (dprobs - inner)
        dbias[a] += dscores
        dsc = dscores.astype(bf16)
        dk_s[rows, :] = (dot(dsc, qs, NN) * scale).astype(bf16)
        dq_s[rows, :] = (gathered(dot(dsc, k, TN)) * scale).astype(bf16)
        return carry

    lax.fori_loop(0, 4, window, 0)

    mix = mix_s[...]
    mq, mk, mv = (dot(normed, d[...], TN) for d in (dq_s, dk_s, dv_s))
    mp = dot(mix, up, TN)
    wide = lambda m, n: jnp.concatenate([m[:, 128:], n[:, :64]], axis=1)
    tiles = (mq[:, :128], wide(mq, mk), mk[:, 64:], mv[:, :128], wide(mv, mp), mp[:, 64:])
    for t, m in enumerate(tiles):
        gw[t * C : (t + 1) * C, :] = m
    dnorm = (
        dot(dq_s[...], wqkv_ref[:, 0:C], NT)
        + dot(dk_s[...], wqkv_ref[:, C : 2 * C], NT)
        + dot(dv_s[...], wqkv_ref[:, 2 * C : 3 * C], NT)
    )
    dgain = jnp.sum(dnorm * xhat, axis=0, keepdims=True)
    high = jnp.concatenate([dgain[:, 128:192], jnp.zeros((1, 64), f32)], axis=1)

    gt[...] = jnp.zeros_like(gt)
    for a in range(2):
        for h in range(HEADS):
            rows = pl.ds((a * HEADS + h) * POS, POS)
            for lon in range(WLON):
                gt[rows, (11 - lon) * POS : (11 - lon) * POS + WIN] += dbias[
                    a, lon * POS : (lon + 1) * POS, h * WIN : (h + 1) * WIN
                ]
    tr[0:WIN] = gt[:, 0:128]
    tr[WIN : 2 * WIN] = gt[:, 128:256]
    tr[2 * WIN :] = jnp.zeros((SHARES * TROWS - 2 * WIN, 128), f32)
    for g in range(6):
        tr[2 * WIN : 2 * WIN + 24, g * 20 : (g + 1) * 20] = gt[g * 24 : (g + 1) * 24, 256:LANES]

    one[GROW:TROW] = jnp.zeros((TROW - GROW, 128), f32)
    for i in range(SHARES):
        one[0:WROWS] = gw[i * WROWS : (i + 1) * WROWS]
        if i < 3:
            one[GROW : GROW + 1] = (dgain[:, :128], high, jnp.zeros((1, 128), f32))[i]
        one[TROW:CHUNK] = tr[i * TROWS : (i + 1) * TROWS]
        grad_ref[i] = one[...].astype(bf16)

    hold(xt, dot(mix, wproj_ref[...], NN).astype(bf16).astype(f32))
    dhat = dnorm * gain_ref[...]
    m1 = jnp.sum(dhat, axis=1, keepdims=True) * (1.0 / C)
    m2 = jnp.sum(dhat * xhat, axis=1, keepdims=True) * (1.0 / C)
    hold(ut, rstd * (dhat - m1 - xhat * m2))
    for lev, lat, w0, w1 in window_parts():
        at = lev * 3 + lat % 3
        first = joined(get(xt, w0), get(ut, w0)).astype(bf16)
        rest = joined(get(xt, w1), get(ut, w1)).astype(bf16)
        near, far = (own_ref, lono_ref) if lat < 3 else (lato_ref, coro_ref)
        near[at * 18 : at * 18 + 12] = first
        near[at * 18 + 12 : (at + 1) * 18] = rest[0:6]
        far[at * 6 : (at + 1) * 6] = rest[6:12]


def run_main(air, up, lonh, lath, corh, gain, wqkv, wproj, bias):
    vmem = pl.BlockSpec(memory_space=pltpu.VMEM)
    tok = lambda dt: pltpu.VMEM((TOK, C), dt)
    return pl.pallas_call(
        main_kernel,
        in_specs=[vmem] * 9,
        out_specs=[vmem] * 5,
        out_shape=[
            HALOS[1],
            *HALOS,
            jax.ShapeDtypeStruct((SHARES, CHUNK, 128), bf16),
        ],
        scratch_shapes=[
            pltpu.VMEM((2 * TOK, 128), f32),
            pltpu.VMEM((2 * TOK, 128), f32),
            pltpu.VMEM((2, WIN, HEADS * WIN), f32),
        ]
        + [tok(bf16)] * 8
        + [
            pltpu.VMEM((SHARES * WROWS, 128), f32),
            pltpu.VMEM((WIN, 384), f32),
            pltpu.VMEM((SHARES * TROWS, 128), f32),
            pltpu.VMEM((CHUNK, 128), f32),
        ],
        compiler_params=pltpu.CompilerParams(vmem_limit_bytes=40 << 20),
        cost_estimate=pl.CostEstimate(flops=10**9, bytes_accessed=4 << 20, transcendentals=0),
        name="sublayer",
    )(air, up, lonh, lath, corh, gain, wqkv, wproj, bias)


def combine_kernel(air_ref, up_ref, own_ref, lonr_ref, latr_ref, corr_ref, out_ref, grad_ref):
    for lev in range(4):
        for r in range(6):
            at = lev * 3 + r % 3
            far, near = (corr_ref, latr_ref) if r < 3 else (lonr_ref, own_ref)
            far = far[at * 6 : (at + 1) * 6].astype(f32)
            near = near[at * 18 : (at + 1) * 18].astype(f32)
            rows = parted(jnp.concatenate([far, near], axis=0))
            for src, dst, row in zip((air_ref, up_ref), (out_ref, grad_ref), rows):
                dst[lev, r] = (src[lev, r].astype(f32) + row).astype(bf16)


def combine(air, up, own, lonr, latr, corr):
    vmem = pl.BlockSpec(memory_space=pltpu.VMEM)
    return pl.pallas_call(
        combine_kernel,
        in_specs=[vmem] * 6,
        out_specs=[vmem] * 2,
        out_shape=[jax.ShapeDtypeStruct(air.shape, bf16)] * 2,
        compiler_params=pltpu.CompilerParams(vmem_limit_bytes=16 << 20),
        cost_estimate=pl.CostEstimate(flops=10**9, bytes_accessed=4 << 20, transcendentals=0),
        name="combine",
    )(air, up, own, lonr, latr, corr)


def unpack_kernel(whole_ref, dwqkv_ref, dwproj_ref, dgain_ref, dtable_ref, gw, tr, gt, flat):
    for i in range(SHARES):
        one = whole_ref[i].astype(f32)
        gw[i * WROWS : (i + 1) * WROWS] = one[0:WROWS]
        tr[i * TROWS : (i + 1) * TROWS] = one[TROW:CHUNK]
        if i == 0:
            dgain_ref[:, :128] = one[GROW : GROW + 1]
        if i == 1:
            dgain_ref[:, 128:] = one[GROW : GROW + 1, :64]
    tiles = [gw[t * C : (t + 1) * C] for t in range(6)]
    for t in range(4):
        dwqkv_ref[:, t * 128 : (t + 1) * 128] = tiles[t]
    dwqkv_ref[:, 512:576] = tiles[4][:, :64]
    dwproj_ref[...] = jnp.concatenate([tiles[4][:, 64:], tiles[5]], axis=1)

    gt[:, 0:128] = tr[0:WIN]
    gt[:, 128:256] = tr[WIN : 2 * WIN]
    gt[:, 256:384] = jnp.zeros((WIN, 128), f32)
    for g in range(6):
        gt[g * 24 : (g + 1) * 24, 256:LANES] = tr[2 * WIN : 2 * WIN + 24, g * 20 : (g + 1) * 20]
    lanes, rows = onehots()
    moved = dot(dot(rows, gt[...].astype(bf16), TN).astype(bf16), lanes, NT)
    for pj in range(POS):
        for pi in range(POS):
            at = (pi * POS + pj) * REL
            flat[:, at : at + REL] = moved[pj * 16 : (pj + 1) * 16, pi * REL : (pi + 1) * REL]
    for h in range(HEADS):
        dtable_ref[h] = flat[2 * h : 2 * h + 2, 0 : POS * POS * REL]


def unpack(whole):
    vmem = pl.BlockSpec(memory_space=pltpu.VMEM)
    return pl.pallas_call(
        unpack_kernel,
        in_specs=[vmem],
        out_specs=[vmem] * 4,
        out_shape=[
            jax.ShapeDtypeStruct((C, 3 * C), f32),
            jax.ShapeDtypeStruct((C, C), f32),
            jax.ShapeDtypeStruct((1, C), f32),
            jax.ShapeDtypeStruct((HEADS, 2, POS * POS * REL), f32),
        ],
        scratch_shapes=[
            pltpu.VMEM((SHARES * WROWS, 128), f32),
            pltpu.VMEM((SHARES * TROWS, 128), f32),
            pltpu.VMEM((WIN, 384), f32),
            pltpu.VMEM((16, 3328), f32),
        ],
        compiler_params=pltpu.CompilerParams(vmem_limit_bytes=16 << 20),
        name="unpack",
    )(whole)


def neighbour(array, lon_by, lat_by):
    lons, lats = lax.axis_size("lon"), lax.axis_size("lat")
    if lat_by == 0:
        return lax.ppermute(array, "lon", [(i, (i + lon_by) % lons) for i in range(lons)])
    if lon_by == 0:
        return lax.ppermute(array, "lat", [(i, (i + lat_by) % lats) for i in range(lats)])
    pairs = [
        (i * lats + j, ((i + lon_by) % lons) * lats + (j + lat_by) % lats)
        for i in range(lons)
        for j in range(lats)
    ]
    return lax.ppermute(array, ("lon", "lat"), pairs)


def each(array, axis):
    copies = jnp.broadcast_to(array, (lax.axis_size(axis), *array.shape))
    return lax.all_to_all(copies, axis, split_axis=0, concat_axis=0, tiled=True)


def summed(array):
    return jnp.sum(array.astype(f32), axis=0).astype(bf16)


def on_device(air, up, gain, wqkv, wproj, table):
    lonh, lath, corh = pack(air, up)
    lath = neighbour(lath, 0, -1)
    lonh = neighbour(lonh, -1, 0)
    corh = neighbour(corh, -1, -1)
    last = (lax.axis_index("lat") == lax.axis_size("lat") - 1).astype(jnp.int32).reshape(1)
    bias = prep(last, table.transpose(0, 2, 1, 3).reshape(HEADS, 2, POS * POS * REL))
    own, lono, lato, coro, grads = run_main(
        air, up, lonh, lath, corh, gain.reshape(1, C), wqkv, wproj, bias
    )
    latr = neighbour(lato, 0, 1)
    lonr = neighbour(lono, 1, 0)
    corr = neighbour(coro, 1, 1)
    part = summed(lax.all_to_all(grads, "lon", split_axis=0, concat_axis=0, tiled=True))
    part, latr, lonr, corr = lax.optimization_barrier((part, latr, lonr, corr))
    weights = summed(each(part[:MID], "lat"))
    share = jnp.concatenate([weights[:TROW], part[TROW:]], axis=0)
    whole = each(share, "lon")
    block_out, d_state = combine(air, up, own, lonr, latr, corr)
    d_wqkv, d_wproj, d_gain, d_table = unpack(whole)
    d_table = d_table.reshape(1, HEADS, 2, POS * POS * REL).transpose(0, 2, 1, 3)
    return (block_out, d_state, d_gain.reshape(C), d_wqkv, d_wproj, d_table)


def solution(mesh):
    grid = P(None, "lat", "lon", None)
    return jax.shard_map(
        on_device,
        mesh=mesh,
        in_specs=(grid, grid, P(), P(), P(), P("lat", None, None, None)),
        out_specs=(grid, grid, P(), P(), P(), P("lat", None, None, None)),
        check_vma=False,
    )
```

```python
import functools

import jax
import jax.numpy as jnp
from jax import lax
from jax.experimental import pallas as pl
from jax.experimental.pallas import tpu as pltpu
from jax.sharding import PartitionSpec as P

HEADS = 6
HEAD = 32
WLEV = 2
WLAT = 6
WLON = 12
WIN = 144
POS = WLEV * WLAT
REL = 2 * WLON - 1
C = 192
TOK = 576
SHARES = 16
WROWS = 72
GROW = 72
TROW = 76
TROWS = 20
CHUNK = 96
MID = 80
LANES = REL * POS

epsilon = 1e-05
masked_score = -1000000000.0
f32 = jnp.float32
bf16 = jnp.bfloat16

NN = (((1,), (0,)), ((), ()))
NT = (((1,), (1,)), ((), ()))
TN = (((0,), (0,)), ((), ()))


def dot(a, b, dims):
    return lax.dot_general(a, b, dims, preferred_element_type=f32)


def window_parts():
    for a in range(2):
        for s in range(WLEV):
            for lat in range(WLAT):
                p = s * WLAT + lat
                yield (2 * a + s + 1) % 4, lat, a * 2 * WIN + p, (a * 2 + 1) * WIN + p


def put(dst, start, rows):
    n = rows.shape[0]
    dst[pl.ds(start, n, stride=POS), :] = rows[:, :128]
    high = jnp.concatenate([rows[:, 128:], jnp.zeros((n, 64), f32)], axis=1)
    dst[pl.ds(TOK + start, n, stride=POS), :] = high


def get(src, start):
    low = src[pl.ds(start, WLON, stride=POS), :]
    high = src[pl.ds(TOK + start, WLON, stride=POS), :]
    return jnp.concatenate([low, high[:, :64]], axis=1)


def whole_rows(src):
    return jnp.concatenate([src[:TOK], src[TOK:][:, :64]], axis=1)


def hold(dst, rows):
    dst[:TOK] = rows[:, :128]
    dst[TOK:, :64] = rows[:, 128:]


def joined(state, up):
    return jnp.concatenate([state[:, :128], up[:, :128], state[:, 128:], up[:, 128:]], axis=1)


def parted(rows):
    state = jnp.concatenate([rows[:, 0:128], rows[:, 256:320]], axis=1)
    return state, jnp.concatenate([rows[:, 128:256], rows[:, 320:384]], axis=1)


def pack_kernel(air_hbm, up_hbm, lonh_ref, lath_ref, corh_ref, low, high, sems):
    copies = []
    for i, src in enumerate((air_hbm, up_hbm)):
        for lev in range(4):
            copies.append(
                pltpu.make_async_copy(src.at[lev, 0:3], low.at[i, lev], sems.at[0, i, lev])
            )
            copies.append(
                pltpu.make_async_copy(
                    src.at[lev, 3:6, 0:8], high.at[i, lev], sems.at[1, i, lev]
                )
            )
    for copy in copies:
        copy.start()
    for copy in copies:
        copy.wait()
    for lev in range(4):
        for r in range(3):
            at = lev * 3 + r
            row = joined(low[0, lev, r].astype(f32), low[1, lev, r].astype(f32)).astype(bf16)
            corh_ref[at * 6 : (at + 1) * 6] = row[0:6]
            lath_ref[at * 18 : (at + 1) * 18] = row[6:24]
            row = joined(high[0, lev, r].astype(f32), high[1, lev, r].astype(f32))
            lonh_ref[at * 6 : (at + 1) * 6] = row.astype(bf16)[0:6]


HALOS = [
    jax.ShapeDtypeStruct((72, 2 * C), bf16),
    jax.ShapeDtypeStruct((216, 2 * C), bf16),
    jax.ShapeDtypeStruct((72, 2 * C), bf16),
]


def pack(air, up):
    vmem = pl.BlockSpec(memory_space=pltpu.VMEM)
    hbm = pl.BlockSpec(memory_space=pltpu.HBM)
    return pl.pallas_call(
        pack_kernel,
        in_specs=[hbm] * 2,
        out_specs=[vmem] * 3,
        out_shape=HALOS,
        scratch_shapes=[
            pltpu.VMEM((2, 4, 3, 24, C), bf16),
            pltpu.VMEM((2, 4, 3, 8, C), bf16),
            pltpu.SemaphoreType.DMA((2, 2, 4)),
        ],
        compiler_params=pltpu.CompilerParams(vmem_limit_bytes=8 << 20),
        name="pack",
    )(
        pltpu.with_memory_space_constraint(air, pltpu.HBM),
        pltpu.with_memory_space_constraint(up, pltpu.HBM),
    )


def normalised(x):
    mean = jnp.sum(x, axis=1, keepdims=True) * (1.0 / C)
    centred = x - mean
    var = jnp.sum(centred * centred, axis=1, keepdims=True) * (1.0 / C)
    rstd = lax.rsqrt(var + epsilon)
    return centred * rstd, rstd


def onehots():
    src = lax.broadcasted_iota(jnp.int32, (384, 384), 0)
    dst = lax.broadcasted_iota(jnp.int32, (384, 384), 1)
    wanted = (dst % POS) * REL + (REL - 1 - dst // POS)
    lanes = ((src == wanted) & (dst < LANES)).astype(f32).astype(bf16)
    to = lax.broadcasted_iota(jnp.int32, (WIN, 192), 0)
    at = lax.broadcasted_iota(jnp.int32, (WIN, 192), 1)
    ah = to // POS
    rows = (at == (to % POS) * 16 + (ah % HEADS) * 2 + ah // HEADS).astype(f32).astype(bf16)
    return lanes, rows


def prep_kernel(last_ref, table_ref, bias, apart, held):
    entries = jnp.concatenate([table_ref[h] for h in range(HEADS)], axis=0)
    apart[...] = jnp.zeros_like(apart)
    for pj in range(POS):
        for pi in range(POS):
            at = (pi * POS + pj) * REL
            apart[pj * 16 : pj * 16 + POS, pi * REL : (pi + 1) * REL] = entries[:, at : at + REL]
    lanes, rows = onehots()
    left = apart[...]
    total = None
    for _ in range(3):
        piece = left.astype(bf16)
        left = left - piece.astype(f32)
        moved = dot(rows, dot(piece, lanes, NN).astype(bf16), NN)
        total = moved if total is None else total + moved
    held[...] = total
    for a in range(2):
        for h in range(HEADS):
            at = (a * HEADS + h) * POS
            for lon in range(WLON):
                bias[a, lon * POS : (lon + 1) * POS, h * WIN : (h + 1) * WIN] = held[
                    at : at + POS, (11 - lon) * POS : (11 - lon) * POS + WIN
                ]
    is_last = last_ref[0]
    for a in range(2):
        pj = lax.broadcasted_iota(jnp.int32, (WIN, 1), 0) % POS
        pi = lax.broadcasted_iota(jnp.int32, (1, HEADS * WIN), 1) % POS

        def region(p):
            lev_part = jnp.where(p >= WLAT, 2 * a, 0)
            lat_part = jnp.where((p % WLAT) >= WLAT // 2, is_last, 0)
            return lev_part + lat_part

        bias[a] = jnp.where(region(pj) == region(pi), bias[a], masked_score)


def prep(last, table):
    vmem = pl.BlockSpec(memory_space=pltpu.VMEM)
    smem = pl.BlockSpec(memory_space=pltpu.SMEM)
    return pl.pallas_call(
        prep_kernel,
        in_specs=[smem, vmem],
        out_specs=vmem,
        out_shape=jax.ShapeDtypeStruct((2, WIN, HEADS * WIN), f32),
        scratch_shapes=[pltpu.VMEM((192, 384), f32), pltpu.VMEM((WIN, 384), f32)],
        compiler_params=pltpu.CompilerParams(vmem_limit_bytes=16 << 20),
        cost_estimate=pl.CostEstimate(flops=10**8, bytes_accessed=2 << 20, transcendentals=0),
        name="prep",
    )(last, table)


def main_kernel(
    air_ref, up_ref, lonh_ref, lath_ref, corh_ref, gain_ref, wqkv_ref, wproj_ref, bias,
    own_ref, lono_ref, lato_ref, coro_ref, grad_ref,
    xt, ut, dbias, q_s, k_s, v_s, dm_s, mix_s, dq_s, dk_s, dv_s, gw, gt, tr, one,
):
    for lev, lat, w0, w1 in window_parts():
        at = lev * 3 + lat % 3
        if lat < 3:
            rows = [src[lev, lat + 3].astype(f32) for src in (air_ref, up_ref)]
            far = parted(lonh_ref[at * 6 : (at + 1) * 6].astype(f32))
            shift = 6
        else:
            rows = parted(lath_ref[at * 18 : (at + 1) * 18].astype(f32))
            far = parted(corh_ref[at * 6 : (at + 1) * 6].astype(f32))
            shift = 0
        for dst, row, edge in zip((xt, ut), rows, far):
            put(dst, w0, row[shift : shift + 12])
            put(dst, w1, row[shift + 12 : shift + 18])
            put(dst, w1 + 72, edge)

    dbias[...] = jnp.zeros_like(dbias)

    x = whole_rows(xt)
    xhat, rstd = normalised(x)
    normed = (xhat * gain_ref[...]).astype(bf16)
    for part, dst in enumerate((q_s, k_s, v_s)):
        dst[...] = dot(normed, wqkv_ref[:, part * C : (part + 1) * C], NN).astype(bf16)
    up = whole_rows(ut).astype(bf16)
    dm_s[...] = dot(up, wproj_ref[...], NT).astype(bf16)

    scale = HEAD**-0.5
    lane_head = lax.broadcasted_iota(jnp.int32, (1, C), 1) // HEAD

    def spread(rows):
        zero = jnp.zeros_like(rows)
        return jnp.concatenate([jnp.where(lane_head == h, rows, zero) for h in range(HEADS)], axis=0)

    def gathered(stacked):
        total = stacked[0:WIN]
        for h in range(1, HEADS):
            total = jnp.where(lane_head == h, stacked[h * WIN : (h + 1) * WIN], total)
        return total

    def window(w):
        a = w // 2
        rows = pl.ds(w * WIN, WIN)
        k, v = k_s[rows, :], v_s[rows, :]
        qs = spread(q_s[rows, :])
        scores = dot(k, qs, NT) * scale + bias[a]
        top = jnp.max(scores, axis=0, keepdims=True)
        weights = jnp.exp(scores - top)
        probs = weights * (1.0 / jnp.sum(weights, axis=0, keepdims=True))
        soft = probs.astype(bf16)
        mix_s[rows, :] = gathered(dot(soft, v, TN)).astype(bf16)
        ds = spread(dm_s[rows, :])
        dprobs = dot(v, ds, NT)
        dv_s[rows, :] = dot(soft, ds, NN).astype(bf16)
        inner = jnp.sum(probs * dprobs, axis=0, keepdims=True)
        dscores = probs * (dprobs - inner)
        dbias[a] += dscores
        dsc = dscores.astype(bf16)
        dk_s[rows, :] = (dot(dsc, qs, NN) * scale).astype(bf16)
        dq_s[rows, :] = (gathered(dot(dsc, k, TN)) * scale).astype(bf16)

    for w in range(4):
        window(w)

    mix = mix_s[...]
    mq, mk, mv = (dot(normed, d[...], TN) for d in (dq_s, dk_s, dv_s))
    mp = dot(mix, up, TN)
    wide = lambda m, n: jnp.concatenate([m[:, 128:], n[:, :64]], axis=1)
    tiles = (mq[:, :128], wide(mq, mk), mk[:, 64:], mv[:, :128], wide(mv, mp), mp[:, 64:])
    for t, m in enumerate(tiles):
        gw[t * C : (t + 1) * C, :] = m
    dnorm = (
        dot(dq_s[...], wqkv_ref[:, 0:C], NT)
        + dot(dk_s[...], wqkv_ref[:, C : 2 * C], NT)
        + dot(dv_s[...], wqkv_ref[:, 2 * C : 3 * C], NT)
    )
    dgain = jnp.sum(dnorm * xhat, axis=0, keepdims=True)
    high = jnp.concatenate([dgain[:, 128:192], jnp.zeros((1, 64), f32)], axis=1)

    gt[...] = jnp.zeros_like(gt)
    for a in range(2):
        for h in range(HEADS):
            rows = pl.ds((a * HEADS + h) * POS, POS)
            for lon in range(WLON):
                gt[rows, (11 - lon) * POS : (11 - lon) * POS + WIN] += dbias[
                    a, lon * POS : (lon + 1) * POS, h * WIN : (h + 1) * WIN
                ]
    tr[0:WIN] = gt[:, 0:128]
    tr[WIN : 2 * WIN] = gt[:, 128:256]
    tr[2 * WIN :] = jnp.zeros((SHARES * TROWS - 2 * WIN, 128), f32)
    for g in range(6):
        tr[2 * WIN : 2 * WIN + 24, g * 20 : (g + 1) * 20] = gt[g * 24 : (g + 1) * 24, 256:LANES]

    one[GROW:TROW] = jnp.zeros((TROW - GROW, 128), f32)
    for i in range(SHARES):
        one[0:WROWS] = gw[i * WROWS : (i + 1) * WROWS]
        if i < 3:
            one[GROW : GROW + 1] = (dgain[:, :128], high, jnp.zeros((1, 128), f32))[i]
        one[TROW:CHUNK] = tr[i * TROWS : (i + 1) * TROWS]
        grad_ref[i] = one[...].astype(bf16)

    hold(xt, dot(mix, wproj_ref[...], NN).astype(bf16).astype(f32))
    dhat = dnorm * gain_ref[...]
    m1 = jnp.sum(dhat, axis=1, keepdims=True) * (1.0 / C)
    m2 = jnp.sum(dhat * xhat, axis=1, keepdims=True) * (1.0 / C)
    hold(ut, rstd * (dhat - m1 - xhat * m2))
    for lev, lat, w0, w1 in window_parts():
        at = lev * 3 + lat % 3
        first = joined(get(xt, w0), get(ut, w0)).astype(bf16)
        rest = joined(get(xt, w1), get(ut, w1)).astype(bf16)
        near, far = (own_ref, lono_ref) if lat < 3 else (lato_ref, coro_ref)
        near[at * 18 : at * 18 + 12] = first
        near[at * 18 + 12 : (at + 1) * 18] = rest[0:6]
        far[at * 6 : (at + 1) * 6] = rest[6:12]


def run_main(air, up, lonh, lath, corh, gain, wqkv, wproj, bias):
    vmem = pl.BlockSpec(memory_space=pltpu.VMEM)
    tok = lambda dt: pltpu.VMEM((TOK, C), dt)
    return pl.pallas_call(
        main_kernel,
        in_specs=[vmem] * 9,
        out_specs=[vmem] * 5,
        out_shape=[
            HALOS[1],
            *HALOS,
            jax.ShapeDtypeStruct((SHARES, CHUNK, 128), bf16),
        ],
        scratch_shapes=[
            pltpu.VMEM((2 * TOK, 128), f32),
            pltpu.VMEM((2 * TOK, 128), f32),
            pltpu.VMEM((2, WIN, HEADS * WIN), f32),
        ]
        + [tok(bf16)] * 8
        + [
            pltpu.VMEM((SHARES * WROWS, 128), f32),
            pltpu.VMEM((WIN, 384), f32),
            pltpu.VMEM((SHARES * TROWS, 128), f32),
            pltpu.VMEM((CHUNK, 128), f32),
        ],
        compiler_params=pltpu.CompilerParams(vmem_limit_bytes=40 << 20),
        cost_estimate=pl.CostEstimate(flops=10**9, bytes_accessed=4 << 20, transcendentals=0),
        name="sublayer",
    )(air, up, lonh, lath, corh, gain, wqkv, wproj, bias)


def combine_kernel(air_ref, up_ref, own_ref, lonr_ref, latr_ref, corr_ref, out_ref, grad_ref):
    for lev in range(4):
        for r in range(6):
            at = lev * 3 + r % 3
            far, near = (corr_ref, latr_ref) if r < 3 else (lonr_ref, own_ref)
            far = far[at * 6 : (at + 1) * 6].astype(f32)
            near = near[at * 18 : (at + 1) * 18].astype(f32)
            rows = parted(jnp.concatenate([far, near], axis=0))
            for src, dst, row in zip((air_ref, up_ref), (out_ref, grad_ref), rows):
                dst[lev, r] = (src[lev, r].astype(f32) + row).astype(bf16)


def combine(air, up, own, lonr, latr, corr):
    vmem = pl.BlockSpec(memory_space=pltpu.VMEM)
    return pl.pallas_call(
        combine_kernel,
        in_specs=[vmem] * 6,
        out_specs=[vmem] * 2,
        out_shape=[jax.ShapeDtypeStruct(air.shape, bf16)] * 2,
        compiler_params=pltpu.CompilerParams(vmem_limit_bytes=16 << 20),
        cost_estimate=pl.CostEstimate(flops=10**10, bytes_accessed=40 << 20, transcendentals=0),
        name="combine",
    )(air, up, own, lonr, latr, corr)


def total(ref):
    parts = [ref[i].astype(f32) for i in range(ref.shape[0])]
    while len(parts) > 1:
        parts = [a + b for a, b in zip(parts[::2], parts[1::2])]
    return parts[0].astype(bf16)


def lon_sum_kernel(parts_ref, copies_ref, table_ref):
    one = total(parts_ref)
    for i in range(copies_ref.shape[0]):
        copies_ref[i] = one[:MID]
    table_ref[...] = one


def lat_sum_kernel(parts_ref, table_ref, copies_ref):
    one = jnp.concatenate([total(parts_ref), table_ref[MID:]], axis=0)
    row = lax.broadcasted_iota(jnp.int32, (CHUNK, 1), 0)
    one = jnp.where(row < TROW, one.astype(f32), table_ref[...].astype(f32)).astype(bf16)
    for i in range(copies_ref.shape[0]):
        copies_ref[i] = one


def lon_sum(parts, lats):
    vmem = pl.BlockSpec(memory_space=pltpu.VMEM)
    return pl.pallas_call(
        lon_sum_kernel,
        in_specs=[vmem],
        out_specs=[vmem] * 2,
        out_shape=[
            jax.ShapeDtypeStruct((lats, MID, 128), bf16),
            jax.ShapeDtypeStruct((CHUNK, 128), bf16),
        ],
        compiler_params=pltpu.CompilerParams(vmem_limit_bytes=4 << 20),
        name="lon_sum",
    )(parts)


def lat_sum(parts, table, lons):
    vmem = pl.BlockSpec(memory_space=pltpu.VMEM)
    return pl.pallas_call(
        lat_sum_kernel,
        in_specs=[vmem] * 2,
        out_specs=vmem,
        out_shape=jax.ShapeDtypeStruct((lons, CHUNK, 128), bf16),
        compiler_params=pltpu.CompilerParams(vmem_limit_bytes=4 << 20),
        name="lat_sum",
    )(parts, table)


def unpack_kernel(whole_ref, dwqkv_ref, dwproj_ref, dgain_ref, dtable_ref, gw, tr, gt, flat):
    for i in range(SHARES):
        one = whole_ref[i].astype(f32)
        gw[i * WROWS : (i + 1) * WROWS] = one[0:WROWS]
        tr[i * TROWS : (i + 1) * TROWS] = one[TROW:CHUNK]
        if i == 0:
            dgain_ref[:, :128] = one[GROW : GROW + 1]
        if i == 1:
            dgain_ref[:, 128:] = one[GROW : GROW + 1, :64]
    tiles = [gw[t * C : (t + 1) * C] for t in range(6)]
    for t in range(4):
        dwqkv_ref[:, t * 128 : (t + 1) * 128] = tiles[t]
    dwqkv_ref[:, 512:576] = tiles[4][:, :64]
    dwproj_ref[...] = jnp.concatenate([tiles[4][:, 64:], tiles[5]], axis=1)

    gt[:, 0:128] = tr[0:WIN]
    gt[:, 128:256] = tr[WIN : 2 * WIN]
    gt[:, 256:384] = jnp.zeros((WIN, 128), f32)
    for g in range(6):
        gt[g * 24 : (g + 1) * 24, 256:LANES] = tr[2 * WIN : 2 * WIN + 24, g * 20 : (g + 1) * 20]
    lanes, rows = onehots()
    moved = dot(dot(rows, gt[...].astype(bf16), TN).astype(bf16), lanes, NT)
    for pj in range(POS):
        for pi in range(POS):
            at = (pi * POS + pj) * REL
            flat[:, at : at + REL] = moved[pj * 16 : (pj + 1) * 16, pi * REL : (pi + 1) * REL]
    for h in range(HEADS):
        dtable_ref[h] = flat[2 * h : 2 * h + 2, 0 : POS * POS * REL]


def unpack(whole):
    vmem = pl.BlockSpec(memory_space=pltpu.VMEM)
    return pl.pallas_call(
        unpack_kernel,
        in_specs=[vmem],
        out_specs=[vmem] * 4,
        out_shape=[
            jax.ShapeDtypeStruct((C, 3 * C), f32),
            jax.ShapeDtypeStruct((C, C), f32),
            jax.ShapeDtypeStruct((1, C), f32),
            jax.ShapeDtypeStruct((HEADS, 2, POS * POS * REL), f32),
        ],
        scratch_shapes=[
            pltpu.VMEM((SHARES * WROWS, 128), f32),
            pltpu.VMEM((SHARES * TROWS, 128), f32),
            pltpu.VMEM((WIN, 384), f32),
            pltpu.VMEM((16, 3328), f32),
        ],
        compiler_params=pltpu.CompilerParams(vmem_limit_bytes=16 << 20),
        name="unpack",
    )(whole)


def neighbour(array, lon_by, lat_by):
    lons, lats = lax.axis_size("lon"), lax.axis_size("lat")
    if lat_by == 0:
        return lax.ppermute(array, "lon", [(i, (i + lon_by) % lons) for i in range(lons)])
    if lon_by == 0:
        return lax.ppermute(array, "lat", [(i, (i + lat_by) % lats) for i in range(lats)])
    pairs = [
        (i * lats + j, ((i + lon_by) % lons) * lats + (j + lat_by) % lats)
        for i in range(lons)
        for j in range(lats)
    ]
    return lax.ppermute(array, ("lon", "lat"), pairs)


def on_device(air, up, gain, wqkv, wproj, table):
    lonh, lath, corh = pack(air, up)
    lath = neighbour(lath, 0, -1)
    lonh = neighbour(lonh, -1, 0)
    corh = neighbour(corh, -1, -1)
    last = (lax.axis_index("lat") == lax.axis_size("lat") - 1).astype(jnp.int32).reshape(1)
    bias = prep(last, table.transpose(0, 2, 1, 3).reshape(HEADS, 2, POS * POS * REL))
    own, lono, lato, coro, grads = run_main(
        air, up, lonh, lath, corh, gain.reshape(1, C), wqkv, wproj, bias
    )
    latr = neighbour(lato, 0, 1)
    lonr = neighbour(lono, 1, 0)
    corr = neighbour(coro, 1, 1)
    parts = lax.all_to_all(grads, "lon", split_axis=0, concat_axis=0, tiled=True)
    copies, table_part = lon_sum(parts, lax.axis_size("lat"))
    parts = lax.all_to_all(copies, "lat", split_axis=0, concat_axis=0, tiled=True)
    copies = lat_sum(parts, table_part, lax.axis_size("lon"))
    whole = lax.all_to_all(copies, "lon", split_axis=0, concat_axis=0, tiled=True)
    block_out, d_state = combine(air, up, own, lonr, latr, corr)
    d_wqkv, d_wproj, d_gain, d_table = unpack(whole)
    d_table = d_table.reshape(1, HEADS, 2, POS * POS * REL).transpose(0, 2, 1, 3)
    return (block_out, d_state, d_gain.reshape(C), d_wqkv, d_wproj, d_table)


def solution(mesh):
    grid = P(None, "lat", "lon", None)
    return jax.shard_map(
        on_device,
        mesh=mesh,
        in_specs=(grid, grid, P(), P(), P(), P("lat", None, None, None)),
        out_specs=(grid, grid, P(), P(), P(), P("lat", None, None, None)),
        check_vma=False,
    )
```

```python
import functools

import jax
import jax.numpy as jnp
from jax import lax
from jax.experimental import pallas as pl
from jax.experimental.pallas import tpu as pltpu
from jax.sharding import Mesh
from jax.sharding import PartitionSpec as P

HEADS = 6
HEAD = 32
WLEV = 2
WLAT = 6
WLON = 12
WIN = 144
POS = WLEV * WLAT
REL = 2 * WLON - 1
C = 192
TOK = 576
SHARES = 16
WROWS = 72
CHUNK = 80
TABLE = 320
LON = ("x", "yh", "core")
LAT = ("yl", "z")
SCATTER = ("yh", "yl", "z")
REST = ("x", "core")
LANES = REL * POS

epsilon = 1e-05
masked_score = -1000000000.0
f32 = jnp.float32
bf16 = jnp.bfloat16

NN = (((1,), (0,)), ((), ()))
NT = (((1,), (1,)), ((), ()))
TN = (((0,), (0,)), ((), ()))


def dot(a, b, dims):
    return lax.dot_general(a, b, dims, preferred_element_type=f32)


def window_parts():
    for a in range(2):
        for s in range(WLEV):
            for lat in range(WLAT):
                p = s * WLAT + lat
                yield (2 * a + s + 1) % 4, lat, a * 2 * WIN + p, (a * 2 + 1) * WIN + p


def put(dst, start, rows):
    n = rows.shape[0]
    dst[pl.ds(start, n, stride=POS), :] = rows[:, :128]
    high = jnp.concatenate([rows[:, 128:], jnp.zeros((n, 64), f32)], axis=1)
    dst[pl.ds(TOK + start, n, stride=POS), :] = high


def get(src, start):
    low = src[pl.ds(start, WLON, stride=POS), :]
    high = src[pl.ds(TOK + start, WLON, stride=POS), :]
    return jnp.concatenate([low, high[:, :64]], axis=1)


def whole_rows(src):
    return jnp.concatenate([src[:TOK], src[TOK:][:, :64]], axis=1)


def hold(dst, rows):
    dst[:TOK] = rows[:, :128]
    dst[TOK:, :64] = rows[:, 128:]


def joined(state, up):
    return jnp.concatenate([state[:, :128], up[:, :128], state[:, 128:], up[:, 128:]], axis=1)


def parted(rows):
    state = jnp.concatenate([rows[:, 0:128], rows[:, 256:320]], axis=1)
    return state, jnp.concatenate([rows[:, 128:256], rows[:, 320:384]], axis=1)


def pack_kernel(air_hbm, up_hbm, lonh_ref, lath_ref, corh_ref, low, high, sems):
    copies = []
    for i, src in enumerate((air_hbm, up_hbm)):
        for lev in range(4):
            copies.append(
                pltpu.make_async_copy(src.at[lev, 0:3], low.at[i, lev], sems.at[0, i, lev])
            )
            copies.append(
                pltpu.make_async_copy(
                    src.at[lev, 3:6, 0:8], high.at[i, lev], sems.at[1, i, lev]
                )
            )
    for copy in copies:
        copy.start()
    for copy in copies:
        copy.wait()
    for lev in range(4):
        for r in range(3):
            at = lev * 3 + r
            row = joined(low[0, lev, r].astype(f32), low[1, lev, r].astype(f32)).astype(bf16)
            corh_ref[at * 6 : (at + 1) * 6] = row[0:6]
            lath_ref[at * 18 : (at + 1) * 18] = row[6:24]
            row = joined(high[0, lev, r].astype(f32), high[1, lev, r].astype(f32))
            lonh_ref[at * 6 : (at + 1) * 6] = row.astype(bf16)[0:6]


HALOS = [
    jax.ShapeDtypeStruct((72, 2 * C), bf16),
    jax.ShapeDtypeStruct((216, 2 * C), bf16),
    jax.ShapeDtypeStruct((72, 2 * C), bf16),
]


def pack(air, up):
    vmem = pl.BlockSpec(memory_space=pltpu.VMEM)
    hbm = pl.BlockSpec(memory_space=pltpu.HBM)
    return pl.pallas_call(
        pack_kernel,
        in_specs=[hbm] * 2,
        out_specs=[vmem] * 3,
        out_shape=HALOS,
        scratch_shapes=[
            pltpu.VMEM((2, 4, 3, 24, C), bf16),
            pltpu.VMEM((2, 4, 3, 8, C), bf16),
            pltpu.SemaphoreType.DMA((2, 2, 4)),
        ],
        compiler_params=pltpu.CompilerParams(vmem_limit_bytes=8 << 20),
        name="pack",
    )(
        pltpu.with_memory_space_constraint(air, pltpu.HBM),
        pltpu.with_memory_space_constraint(up, pltpu.HBM),
    )


def normalised(x):
    mean = jnp.sum(x, axis=1, keepdims=True) * (1.0 / C)
    centred = x - mean
    var = jnp.sum(centred * centred, axis=1, keepdims=True) * (1.0 / C)
    rstd = lax.rsqrt(var + epsilon)
    return centred * rstd, rstd


def onehots():
    src = lax.broadcasted_iota(jnp.int32, (384, 384), 0)
    dst = lax.broadcasted_iota(jnp.int32, (384, 384), 1)
    wanted = (dst % POS) * REL + (REL - 1 - dst // POS)
    lanes = ((src == wanted) & (dst < LANES)).astype(f32).astype(bf16)
    to = lax.broadcasted_iota(jnp.int32, (WIN, 192), 0)
    at = lax.broadcasted_iota(jnp.int32, (WIN, 192), 1)
    ah = to // POS
    rows = (at == (to % POS) * 16 + (ah % HEADS) * 2 + ah // HEADS).astype(f32).astype(bf16)
    return lanes, rows


def prep_kernel(last_ref, table_ref, bias, apart, held):
    entries = jnp.concatenate([table_ref[h] for h in range(HEADS)], axis=0)
    apart[...] = jnp.zeros_like(apart)
    for pj in range(POS):
        for pi in range(POS):
            at = (pi * POS + pj) * REL
            apart[pj * 16 : pj * 16 + POS, pi * REL : (pi + 1) * REL] = entries[:, at : at + REL]
    lanes, rows = onehots()
    left = apart[...]
    total = None
    for _ in range(3):
        piece = left.astype(bf16)
        left = left - piece.astype(f32)
        moved = dot(rows, dot(piece, lanes, NN).astype(bf16), NN)
        total = moved if total is None else total + moved
    held[...] = total
    for a in range(2):
        for h in range(HEADS):
            at = (a * HEADS + h) * POS
            for lon in range(WLON):
                bias[a, lon * POS : (lon + 1) * POS, h * WIN : (h + 1) * WIN] = held[
                    at : at + POS, (11 - lon) * POS : (11 - lon) * POS + WIN
                ]
    is_last = last_ref[0]
    for a in range(2):
        pj = lax.broadcasted_iota(jnp.int32, (WIN, 1), 0) % POS
        pi = lax.broadcasted_iota(jnp.int32, (1, HEADS * WIN), 1) % POS

        def region(p):
            lev_part = jnp.where(p >= WLAT, 2 * a, 0)
            lat_part = jnp.where((p % WLAT) >= WLAT // 2, is_last, 0)
            return lev_part + lat_part

        bias[a] = jnp.where(region(pj) == region(pi), bias[a], masked_score)


def prep(last, table):
    vmem = pl.BlockSpec(memory_space=pltpu.VMEM)
    smem = pl.BlockSpec(memory_space=pltpu.SMEM)
    return pl.pallas_call(
        prep_kernel,
        in_specs=[smem, vmem],
        out_specs=vmem,
        out_shape=jax.ShapeDtypeStruct((2, WIN, HEADS * WIN), f32),
        scratch_shapes=[pltpu.VMEM((192, 384), f32), pltpu.VMEM((WIN, 384), f32)],
        compiler_params=pltpu.CompilerParams(vmem_limit_bytes=16 << 20),
        cost_estimate=pl.CostEstimate(flops=10**8, bytes_accessed=2 << 20, transcendentals=0),
        name="prep",
    )(last, table)


def main_kernel(
    air_ref, up_ref, lonh_ref, lath_ref, corh_ref, gain_ref, wqkv_ref, wproj_ref, bias,
    own_ref, lono_ref, lato_ref, coro_ref, grad_ref, table_ref,
    xt, ut, dbias, q_s, k_s, v_s, dm_s, mix_s, dq_s, dk_s, dv_s, gw, gt, tr, one,
):
    for lev, lat, w0, w1 in window_parts():
        at = lev * 3 + lat % 3
        if lat < 3:
            rows = [src[lev, lat + 3].astype(f32) for src in (air_ref, up_ref)]
            far = parted(lonh_ref[at * 6 : (at + 1) * 6].astype(f32))
            shift = 6
        else:
            rows = parted(lath_ref[at * 18 : (at + 1) * 18].astype(f32))
            far = parted(corh_ref[at * 6 : (at + 1) * 6].astype(f32))
            shift = 0
        for dst, row, edge in zip((xt, ut), rows, far):
            put(dst, w0, row[shift : shift + 12])
            put(dst, w1, row[shift + 12 : shift + 18])
            put(dst, w1 + 72, edge)

    dbias[...] = jnp.zeros_like(dbias)

    x = whole_rows(xt)
    xhat, rstd = normalised(x)
    normed = (xhat * gain_ref[...]).astype(bf16)
    for part, dst in enumerate((q_s, k_s, v_s)):
        dst[...] = dot(normed, wqkv_ref[:, part * C : (part + 1) * C], NN).astype(bf16)
    up = whole_rows(ut).astype(bf16)
    dm_s[...] = dot(up, wproj_ref[...], NT).astype(bf16)

    scale = HEAD**-0.5
    lane_head = lax.broadcasted_iota(jnp.int32, (1, C), 1) // HEAD

    def spread(rows):
        zero = jnp.zeros_like(rows)
        return jnp.concatenate([jnp.where(lane_head == h, rows, zero) for h in range(HEADS)], axis=0)

    def gathered(stacked):
        total = stacked[0:WIN]
        for h in range(1, HEADS):
            total = jnp.where(lane_head == h, stacked[h * WIN : (h + 1) * WIN], total)
        return total

    def window(w):
        a = w // 2
        rows = pl.ds(w * WIN, WIN)
        k, v = k_s[rows, :], v_s[rows, :]
        qs = spread(q_s[rows, :])
        scores = dot(k, qs, NT) * scale + bias[a]
        top = jnp.max(scores, axis=0, keepdims=True)
        weights = jnp.exp(scores - top)
        probs = weights * (1.0 / jnp.sum(weights, axis=0, keepdims=True))
        soft = probs.astype(bf16)
        mix_s[rows, :] = gathered(dot(soft, v, TN)).astype(bf16)
        ds = spread(dm_s[rows, :])
        dprobs = dot(v, ds, NT)
        dv_s[rows, :] = dot(soft, ds, NN).astype(bf16)
        inner = jnp.sum(probs * dprobs, axis=0, keepdims=True)
        dscores = probs * (dprobs - inner)
        dbias[a] += dscores
        dsc = dscores.astype(bf16)
        dk_s[rows, :] = (dot(dsc, qs, NN) * scale).astype(bf16)
        dq_s[rows, :] = (gathered(dot(dsc, k, TN)) * scale).astype(bf16)

    for w in range(4):
        window(w)

    mix = mix_s[...]
    mq, mk, mv = (dot(normed, d[...], TN) for d in (dq_s, dk_s, dv_s))
    mp = dot(mix, up, TN)
    wide = lambda m, n: jnp.concatenate([m[:, 128:], n[:, :64]], axis=1)
    tiles = (mq[:, :128], wide(mq, mk), mk[:, 64:], mv[:, :128], wide(mv, mp), mp[:, 64:])
    for t, m in enumerate(tiles):
        gw[t * C : (t + 1) * C, :] = m
    dnorm = (
        dot(dq_s[...], wqkv_ref[:, 0:C], NT)
        + dot(dk_s[...], wqkv_ref[:, C : 2 * C], NT)
        + dot(dv_s[...], wqkv_ref[:, 2 * C : 3 * C], NT)
    )
    dgain = jnp.sum(dnorm * xhat, axis=0, keepdims=True)
    high = jnp.concatenate([dgain[:, 128:192], jnp.zeros((1, 64), f32)], axis=1)

    gt[...] = jnp.zeros_like(gt)
    for a in range(2):
        for h in range(HEADS):
            rows = pl.ds((a * HEADS + h) * POS, POS)
            for lon in range(WLON):
                gt[rows, (11 - lon) * POS : (11 - lon) * POS + WIN] += dbias[
                    a, lon * POS : (lon + 1) * POS, h * WIN : (h + 1) * WIN
                ]
    tr[0:WIN] = gt[:, 0:128]
    tr[WIN : 2 * WIN] = gt[:, 128:256]
    tr[2 * WIN :] = jnp.zeros((TABLE - 2 * WIN, 128), f32)
    for g in range(6):
        tr[2 * WIN : 2 * WIN + 24, g * 20 : (g + 1) * 20] = gt[g * 24 : (g + 1) * 24, 256:LANES]

    table_ref[...] = tr[...].astype(bf16)
    one[WROWS:CHUNK] = jnp.zeros((CHUNK - WROWS, 128), f32)
    for i in range(SHARES):
        one[0:WROWS] = gw[i * WROWS : (i + 1) * WROWS]
        if i < 3:
            one[WROWS : WROWS + 1] = (dgain[:, :128], high, jnp.zeros((1, 128), f32))[i]
        grad_ref[i] = one[...].astype(bf16)

    hold(xt, dot(mix, wproj_ref[...], NN).astype(bf16).astype(f32))
    dhat = dnorm * gain_ref[...]
    m1 = jnp.sum(dhat, axis=1, keepdims=True) * (1.0 / C)
    m2 = jnp.sum(dhat * xhat, axis=1, keepdims=True) * (1.0 / C)
    hold(ut, rstd * (dhat - m1 - xhat * m2))
    for lev, lat, w0, w1 in window_parts():
        at = lev * 3 + lat % 3
        first = joined(get(xt, w0), get(ut, w0)).astype(bf16)
        rest = joined(get(xt, w1), get(ut, w1)).astype(bf16)
        near, far = (own_ref, lono_ref) if lat < 3 else (lato_ref, coro_ref)
        near[at * 18 : at * 18 + 12] = first
        near[at * 18 + 12 : (at + 1) * 18] = rest[0:6]
        far[at * 6 : (at + 1) * 6] = rest[6:12]


def run_main(air, up, lonh, lath, corh, gain, wqkv, wproj, bias):
    vmem = pl.BlockSpec(memory_space=pltpu.VMEM)
    tok = lambda dt: pltpu.VMEM((TOK, C), dt)
    return pl.pallas_call(
        main_kernel,
        in_specs=[vmem] * 9,
        out_specs=[vmem] * 6,
        out_shape=[
            HALOS[1],
            *HALOS,
            jax.ShapeDtypeStruct((SHARES, CHUNK, 128), bf16),
            jax.ShapeDtypeStruct((TABLE, 128), bf16),
        ],
        scratch_shapes=[
            pltpu.VMEM((2 * TOK, 128), f32),
            pltpu.VMEM((2 * TOK, 128), f32),
            pltpu.VMEM((2, WIN, HEADS * WIN), f32),
        ]
        + [tok(bf16)] * 8
        + [
            pltpu.VMEM((SHARES * WROWS, 128), f32),
            pltpu.VMEM((WIN, 384), f32),
            pltpu.VMEM((TABLE, 128), f32),
            pltpu.VMEM((CHUNK, 128), f32),
        ],
        compiler_params=pltpu.CompilerParams(vmem_limit_bytes=40 << 20),
        cost_estimate=pl.CostEstimate(flops=10**9, bytes_accessed=4 << 20, transcendentals=0),
        name="sublayer",
    )(air, up, lonh, lath, corh, gain, wqkv, wproj, bias)


def combine_kernel(air_ref, up_ref, own_ref, lonr_ref, latr_ref, corr_ref, out_ref, grad_ref):
    for lev in range(4):
        for r in range(6):
            at = lev * 3 + r % 3
            far, near = (corr_ref, latr_ref) if r < 3 else (lonr_ref, own_ref)
            far = far[at * 6 : (at + 1) * 6].astype(f32)
            near = near[at * 18 : (at + 1) * 18].astype(f32)
            rows = parted(jnp.concatenate([far, near], axis=0))
            for src, dst, row in zip((air_ref, up_ref), (out_ref, grad_ref), rows):
                dst[lev, r] = (src[lev, r].astype(f32) + row).astype(bf16)


def combine(air, up, own, lonr, latr, corr):
    vmem = pl.BlockSpec(memory_space=pltpu.VMEM)
    return pl.pallas_call(
        combine_kernel,
        in_specs=[vmem] * 6,
        out_specs=[vmem] * 2,
        out_shape=[jax.ShapeDtypeStruct(air.shape, bf16)] * 2,
        compiler_params=pltpu.CompilerParams(vmem_limit_bytes=16 << 20),
        cost_estimate=pl.CostEstimate(flops=10**10, bytes_accessed=40 << 20, transcendentals=0),
        name="combine",
    )(air, up, own, lonr, latr, corr)


def total(ref):
    parts = [ref[i].astype(f32) for i in range(ref.shape[0])]
    while len(parts) > 1:
        parts = [a + b for a, b in zip(parts[::2], parts[1::2])]
    return parts[0].astype(bf16)


def sum_kernel(*refs):
    carried = (len(refs) - 2) // 2
    parts_ref, copies_ref = refs[0], refs[1 + carried]
    one = total(parts_ref)
    for i in range(copies_ref.shape[0]):
        copies_ref[i] = one


def summed(parts, copies, *carried):
    vmem = pl.BlockSpec(memory_space=pltpu.VMEM)
    anywhere = pl.BlockSpec(memory_space=pl.ANY)
    return pl.pallas_call(
        sum_kernel,
        in_specs=[vmem] + [anywhere] * len(carried),
        out_specs=[vmem] + [anywhere] * len(carried),
        out_shape=[jax.ShapeDtypeStruct((copies, CHUNK, 128), bf16)]
        + [jax.ShapeDtypeStruct(array.shape, array.dtype) for array in carried],
        input_output_aliases={1 + i: 1 + i for i in range(len(carried))},
        compiler_params=pltpu.CompilerParams(vmem_limit_bytes=4 << 20),
        name="summed",
    )(parts, *carried)


def unpack_kernel(whole_ref, dwqkv_ref, dwproj_ref, dgain_ref, gw):
    for i in range(SHARES):
        one = whole_ref[i].astype(f32)
        gw[i * WROWS : (i + 1) * WROWS] = one[0:WROWS]
        if i == 0:
            dgain_ref[:, :128] = one[WROWS : WROWS + 1]
        if i == 1:
            dgain_ref[:, 128:] = one[WROWS : WROWS + 1, :64]
    tiles = [gw[t * C : (t + 1) * C] for t in range(6)]
    for t in range(4):
        dwqkv_ref[:, t * 128 : (t + 1) * 128] = tiles[t]
    dwqkv_ref[:, 512:576] = tiles[4][:, :64]
    dwproj_ref[...] = jnp.concatenate([tiles[4][:, 64:], tiles[5]], axis=1)


def unpack(whole):
    vmem = pl.BlockSpec(memory_space=pltpu.VMEM)
    return pl.pallas_call(
        unpack_kernel,
        in_specs=[vmem],
        out_specs=[vmem] * 3,
        out_shape=[
            jax.ShapeDtypeStruct((C, 3 * C), f32),
            jax.ShapeDtypeStruct((C, C), f32),
            jax.ShapeDtypeStruct((1, C), f32),
        ],
        scratch_shapes=[pltpu.VMEM((SHARES * WROWS, 128), f32)],
        compiler_params=pltpu.CompilerParams(vmem_limit_bytes=16 << 20),
        name="unpack",
    )(whole)


def turn_kernel(tr, dtable_ref, gt, flat):
    gt[:, 0:128] = tr[0:WIN].astype(f32)
    gt[:, 128:256] = tr[WIN : 2 * WIN].astype(f32)
    gt[:, 256:384] = jnp.zeros((WIN, 128), f32)
    last = tr[2 * WIN :].astype(f32)
    for g in range(6):
        gt[g * 24 : (g + 1) * 24, 256:LANES] = last[:24, g * 20 : (g + 1) * 20]
    lanes, rows = onehots()
    moved = dot(dot(rows, gt[...].astype(bf16), TN).astype(bf16), lanes, NT)
    for pj in range(POS):
        for pi in range(POS):
            at = (pi * POS + pj) * REL
            flat[:, at : at + REL] = moved[pj * 16 : (pj + 1) * 16, pi * REL : (pi + 1) * REL]
    for h in range(HEADS):
        dtable_ref[h] = flat[2 * h : 2 * h + 2, 0 : POS * POS * REL]


def turned(table):
    vmem = pl.BlockSpec(memory_space=pltpu.VMEM)
    return pl.pallas_call(
        turn_kernel,
        in_specs=[vmem],
        out_specs=vmem,
        out_shape=jax.ShapeDtypeStruct((HEADS, 2, POS * POS * REL), f32),
        scratch_shapes=[pltpu.VMEM((WIN, 384), f32), pltpu.VMEM((16, 3328), f32)],
        compiler_params=pltpu.CompilerParams(vmem_limit_bytes=8 << 20),
        cost_estimate=pl.CostEstimate(flops=10**9, bytes_accessed=4 << 20, transcendentals=0),
        name="turn",
    )(table)


def pairs_of(mesh_shape, lon_by, lat_by):
    lons, lats = (mesh_shape[0], mesh_shape[1])
    return [
        (i * lats + j, ((i + lon_by) % lons) * lats + (j + lat_by) % lats)
        for i in range(lons)
        for j in range(lats)
    ]


def on_device(lons, lats, air, up, gain, wqkv, wproj, table):
    def neighbour(array, lon_by, lat_by):
        if lat_by == 0:
            return lax.ppermute(array, LON, [(i, (i + lon_by) % lons) for i in range(lons)])
        if lon_by == 0:
            return lax.ppermute(array, LAT, [(i, (i + lat_by) % lats) for i in range(lats)])
        return lax.ppermute(array, LON + LAT, pairs_of((lons, lats), lon_by, lat_by))

    lonh, lath, corh = pack(air, up)
    lath = neighbour(lath, 0, -1)
    lonh = neighbour(lonh, -1, 0)
    corh = neighbour(corh, -1, -1)
    last = (lax.axis_index(LAT) == lats - 1).astype(jnp.int32).reshape(1)
    bias = prep(last, table.transpose(0, 2, 1, 3).reshape(HEADS, 2, POS * POS * REL))
    own, lono, lato, coro, grads, entries = run_main(
        air, up, lonh, lath, corh, gain.reshape(1, C), wqkv, wproj, bias
    )
    def paired(entries, step):
        other = lax.ppermute(entries, LON, [(i, i ^ step) for i in range(lons)])
        return (entries.astype(f32) + other.astype(f32)).astype(bf16)

    parts = lax.all_to_all(grads, SCATTER, split_axis=0, concat_axis=0, tiled=True)
    copies, entries, lato, lono, coro = summed(parts, 8, entries, lato, lono, coro)
    parts = lax.all_to_all(copies, REST, split_axis=0, concat_axis=0, tiled=True)
    latr = neighbour(lato, 0, 1)
    lonr = neighbour(lono, 1, 0)
    corr = neighbour(coro, 1, 1)
    for step in (1, 2, 4):
        entries = paired(entries, step)
    (copies,) = summed(parts, SHARES)
    whole = lax.all_to_all(copies, SCATTER, split_axis=0, concat_axis=0, tiled=True)
    entries = paired(entries, 8)
    d_table = turned(entries)
    block_out, d_state = combine(air, up, own, lonr, latr, corr)
    d_wqkv, d_wproj, d_gain = unpack(whole)
    d_table = d_table.reshape(1, HEADS, 2, POS * POS * REL).transpose(0, 2, 1, 3)
    return (block_out, d_state, d_gain.reshape(C), d_wqkv, d_wproj, d_table)


def solution(mesh):
    fine = Mesh(mesh.devices.reshape(4, 2, 2, 2, 4), LON + LAT)
    grid = P(None, LAT, LON, None)
    return jax.shard_map(
        functools.partial(on_device, mesh.shape["lon"], mesh.shape["lat"]),
        mesh=fine,
        in_specs=(grid, grid, P(), P(), P(), P(LAT, None, None, None)),
        out_specs=(grid, grid, P(), P(), P(), P(LAT, None, None, None)),
        check_vma=False,
    )
```

```python
import functools

import jax
import jax.numpy as jnp
from jax import lax
from jax.experimental import pallas as pl
from jax.experimental.pallas import tpu as pltpu
from jax.sharding import Mesh
from jax.sharding import PartitionSpec as P

HEADS = 6
HEAD = 32
WLEV = 2
WLAT = 6
WLON = 12
WIN = 144
POS = WLEV * WLAT
REL = 2 * WLON - 1
C = 192
TOK = 576
SHARES = 16
WROWS = 72
CHUNK = 80
TABLE = 320
LON = ("x", "yh", "core")
LAT = ("yl", "z")
SCATTER = ("yh", "yl", "z")
REST = ("x", "core")
LANES = REL * POS

epsilon = 1e-05
masked_score = -1000000000.0
f32 = jnp.float32
bf16 = jnp.bfloat16

NN = (((1,), (0,)), ((), ()))
NT = (((1,), (1,)), ((), ()))
TN = (((0,), (0,)), ((), ()))


def dot(a, b, dims):
    return lax.dot_general(a, b, dims, preferred_element_type=f32)


def window_parts():
    for a in range(2):
        for s in range(WLEV):
            for lat in range(WLAT):
                p = s * WLAT + lat
                yield (2 * a + s + 1) % 4, lat, a * 2 * WIN + p, (a * 2 + 1) * WIN + p


def put(dst, start, rows):
    n = rows.shape[0]
    dst[pl.ds(start, n, stride=POS), :] = rows[:, :128]
    high = jnp.concatenate([rows[:, 128:], jnp.zeros((n, 64), f32)], axis=1)
    dst[pl.ds(TOK + start, n, stride=POS), :] = high


def get(src, start):
    low = src[pl.ds(start, WLON, stride=POS), :]
    high = src[pl.ds(TOK + start, WLON, stride=POS), :]
    return jnp.concatenate([low, high[:, :64]], axis=1)


def whole_rows(src):
    return jnp.concatenate([src[:TOK], src[TOK:][:, :64]], axis=1)


def hold(dst, rows):
    dst[:TOK] = rows[:, :128]
    dst[TOK:, :64] = rows[:, 128:]


def joined(state, up):
    return jnp.concatenate([state[:, :128], up[:, :128], state[:, 128:], up[:, 128:]], axis=1)


def parted(rows):
    state = jnp.concatenate([rows[:, 0:128], rows[:, 256:320]], axis=1)
    return state, jnp.concatenate([rows[:, 128:256], rows[:, 320:384]], axis=1)


def pack_kernel(air_hbm, up_hbm, lonh_ref, lath_ref, corh_ref, low, high, sems):
    copies = []
    for i, src in enumerate((air_hbm, up_hbm)):
        for lev in range(4):
            copies.append(
                pltpu.make_async_copy(src.at[lev, 0:3], low.at[i, lev], sems.at[0, i, lev])
            )
            copies.append(
                pltpu.make_async_copy(
                    src.at[lev, 3:6, 0:8], high.at[i, lev], sems.at[1, i, lev]
                )
            )
    for copy in copies:
        copy.start()
    for copy in copies:
        copy.wait()
    for lev in range(4):
        for r in range(3):
            at = lev * 3 + r
            row = joined(low[0, lev, r].astype(f32), low[1, lev, r].astype(f32)).astype(bf16)
            corh_ref[at * 6 : (at + 1) * 6] = row[0:6]
            lath_ref[at * 18 : (at + 1) * 18] = row[6:24]
            row = joined(high[0, lev, r].astype(f32), high[1, lev, r].astype(f32))
            lonh_ref[at * 6 : (at + 1) * 6] = row.astype(bf16)[0:6]


HALOS = [
    jax.ShapeDtypeStruct((72, 2 * C), bf16),
    jax.ShapeDtypeStruct((216, 2 * C), bf16),
    jax.ShapeDtypeStruct((72, 2 * C), bf16),
]


def pack(air, up):
    vmem = pl.BlockSpec(memory_space=pltpu.VMEM)
    hbm = pl.BlockSpec(memory_space=pltpu.HBM)
    return pl.pallas_call(
        pack_kernel,
        in_specs=[hbm] * 2,
        out_specs=[vmem] * 3,
        out_shape=HALOS,
        scratch_shapes=[
            pltpu.VMEM((2, 4, 3, 24, C), bf16),
            pltpu.VMEM((2, 4, 3, 8, C), bf16),
            pltpu.SemaphoreType.DMA((2, 2, 4)),
        ],
        compiler_params=pltpu.CompilerParams(vmem_limit_bytes=8 << 20),
        name="pack",
    )(
        pltpu.with_memory_space_constraint(air, pltpu.HBM),
        pltpu.with_memory_space_constraint(up, pltpu.HBM),
    )


def normalised(x):
    mean = jnp.sum(x, axis=1, keepdims=True) * (1.0 / C)
    centred = x - mean
    var = jnp.sum(centred * centred, axis=1, keepdims=True) * (1.0 / C)
    rstd = lax.rsqrt(var + epsilon)
    return centred * rstd, rstd


def onehots():
    src = lax.broadcasted_iota(jnp.int32, (384, 384), 0)
    dst = lax.broadcasted_iota(jnp.int32, (384, 384), 1)
    wanted = (dst % POS) * REL + (REL - 1 - dst // POS)
    lanes = ((src == wanted) & (dst < LANES)).astype(f32).astype(bf16)
    to = lax.broadcasted_iota(jnp.int32, (WIN, 192), 0)
    at = lax.broadcasted_iota(jnp.int32, (WIN, 192), 1)
    ah = to // POS
    rows = (at == (to % POS) * 16 + (ah % HEADS) * 2 + ah // HEADS).astype(f32).astype(bf16)
    return lanes, rows


def prep_kernel(last_ref, table_ref, bias, apart, held):
    entries = jnp.concatenate([table_ref[h] for h in range(HEADS)], axis=0)
    apart[...] = jnp.zeros_like(apart)
    for pj in range(POS):
        for pi in range(POS):
            at = (pi * POS + pj) * REL
            apart[pj * 16 : pj * 16 + POS, pi * REL : (pi + 1) * REL] = entries[:, at : at + REL]
    lanes, rows = onehots()
    left = apart[...]
    total = None
    for _ in range(3):
        piece = left.astype(bf16)
        left = left - piece.astype(f32)
        moved = dot(rows, dot(piece, lanes, NN).astype(bf16), NN)
        total = moved if total is None else total + moved
    held[...] = total
    for a in range(2):
        for h in range(HEADS):
            at = (a * HEADS + h) * POS
            for lon in range(WLON):
                bias[a, lon * POS : (lon + 1) * POS, h * WIN : (h + 1) * WIN] = held[
                    at : at + POS, (11 - lon) * POS : (11 - lon) * POS + WIN
                ]
    is_last = last_ref[0]
    for a in range(2):
        pj = lax.broadcasted_iota(jnp.int32, (WIN, 1), 0) % POS
        pi = lax.broadcasted_iota(jnp.int32, (1, HEADS * WIN), 1) % POS

        def region(p):
            lev_part = jnp.where(p >= WLAT, 2 * a, 0)
            lat_part = jnp.where((p % WLAT) >= WLAT // 2, is_last, 0)
            return lev_part + lat_part

        bias[a] = jnp.where(region(pj) == region(pi), bias[a], masked_score)


def prep(last, table):
    vmem = pl.BlockSpec(memory_space=pltpu.VMEM)
    smem = pl.BlockSpec(memory_space=pltpu.SMEM)
    return pl.pallas_call(
        prep_kernel,
        in_specs=[smem, vmem],
        out_specs=vmem,
        out_shape=jax.ShapeDtypeStruct((2, WIN, HEADS * WIN), f32),
        scratch_shapes=[pltpu.VMEM((192, 384), f32), pltpu.VMEM((WIN, 384), f32)],
        compiler_params=pltpu.CompilerParams(vmem_limit_bytes=16 << 20),
        cost_estimate=pl.CostEstimate(flops=10**8, bytes_accessed=2 << 20, transcendentals=0),
        name="prep",
    )(last, table)


def main_kernel(
    air_ref, up_ref, lonh_ref, lath_ref, corh_ref, gain_ref, wqkv_ref, wproj_ref, bias,
    own_ref, lono_ref, lato_ref, coro_ref, grad_ref, table_ref,
    xt, ut, dbias, q_s, k_s, v_s, dm_s, mix_s, dq_s, dk_s, dv_s, gw, gt, tr, one,
):
    for lev, lat, w0, w1 in window_parts():
        at = lev * 3 + lat % 3
        if lat < 3:
            rows = [src[lev, lat + 3].astype(f32) for src in (air_ref, up_ref)]
            far = parted(lonh_ref[at * 6 : (at + 1) * 6].astype(f32))
            shift = 6
        else:
            rows = parted(lath_ref[at * 18 : (at + 1) * 18].astype(f32))
            far = parted(corh_ref[at * 6 : (at + 1) * 6].astype(f32))
            shift = 0
        for dst, row, edge in zip((xt, ut), rows, far):
            put(dst, w0, row[shift : shift + 12])
            put(dst, w1, row[shift + 12 : shift + 18])
            put(dst, w1 + 72, edge)

    dbias[...] = jnp.zeros_like(dbias)

    x = whole_rows(xt)
    xhat, rstd = normalised(x)
    normed = (xhat * gain_ref[...]).astype(bf16)
    for part, dst in enumerate((q_s, k_s, v_s)):
        dst[...] = dot(normed, wqkv_ref[:, part * C : (part + 1) * C], NN).astype(bf16)
    up = whole_rows(ut).astype(bf16)
    dm_s[...] = dot(up, wproj_ref[...], NT).astype(bf16)

    scale = HEAD**-0.5
    lane_head = lax.broadcasted_iota(jnp.int32, (1, C), 1) // HEAD

    def spread(rows):
        zero = jnp.zeros_like(rows)
        return jnp.concatenate([jnp.where(lane_head == h, rows, zero) for h in range(HEADS)], axis=0)

    def gathered(stacked):
        total = stacked[0:WIN]
        for h in range(1, HEADS):
            total = jnp.where(lane_head == h, stacked[h * WIN : (h + 1) * WIN], total)
        return total

    def begin(w):
        rows = pl.ds(w * WIN, WIN)
        qs = spread(q_s[rows, :])
        scores = dot(k_s[rows, :], qs, NT)
        return rows, qs, scores, dot(v_s[rows, :], spread(dm_s[rows, :]), NT)

    def middle(w, state):
        rows, qs, scores, dprobs = state
        a = w // 2
        scores = scores * scale + bias[a]
        top = jnp.max(scores, axis=0, keepdims=True)
        weights = jnp.exp(scores - top)
        probs = weights * (1.0 / jnp.sum(weights, axis=0, keepdims=True))
        inner = jnp.sum(probs * dprobs, axis=0, keepdims=True)
        dscores = probs * (dprobs - inner)
        dbias[a] += dscores
        return rows, qs, probs.astype(bf16), dscores.astype(bf16)

    def end(w, state):
        rows, qs, soft, dsc = state
        mix_s[rows, :] = gathered(dot(soft, v_s[rows, :], TN)).astype(bf16)
        dv_s[rows, :] = dot(soft, spread(dm_s[rows, :]), NN).astype(bf16)
        dk_s[rows, :] = (dot(dsc, qs, NN) * scale).astype(bf16)
        dq_s[rows, :] = (gathered(dot(dsc, k_s[rows, :], TN)) * scale).astype(bf16)

    ready = begin(0)
    for w in range(4):
        done = middle(w, ready)
        if w < 3:
            ready = begin(w + 1)
        end(w, done)

    mix = mix_s[...]
    mq, mk, mv = (dot(normed, d[...], TN) for d in (dq_s, dk_s, dv_s))
    mp = dot(mix, up, TN)
    wide = lambda m, n: jnp.concatenate([m[:, 128:], n[:, :64]], axis=1)
    tiles = (mq[:, :128], wide(mq, mk), mk[:, 64:], mv[:, :128], wide(mv, mp), mp[:, 64:])
    for t, m in enumerate(tiles):
        gw[t * C : (t + 1) * C, :] = m
    dnorm = (
        dot(dq_s[...], wqkv_ref[:, 0:C], NT)
        + dot(dk_s[...], wqkv_ref[:, C : 2 * C], NT)
        + dot(dv_s[...], wqkv_ref[:, 2 * C : 3 * C], NT)
    )
    dgain = jnp.sum(dnorm * xhat, axis=0, keepdims=True)
    high = jnp.concatenate([dgain[:, 128:192], jnp.zeros((1, 64), f32)], axis=1)

    gt[...] = jnp.zeros_like(gt)
    for a in range(2):
        for h in range(HEADS):
            rows = pl.ds((a * HEADS + h) * POS, POS)
            for lon in range(WLON):
                gt[rows, (11 - lon) * POS : (11 - lon) * POS + WIN] += dbias[
                    a, lon * POS : (lon + 1) * POS, h * WIN : (h + 1) * WIN
                ]
    tr[0:WIN] = gt[:, 0:128]
    tr[WIN : 2 * WIN] = gt[:, 128:256]
    tr[2 * WIN :] = jnp.zeros((TABLE - 2 * WIN, 128), f32)
    for g in range(6):
        tr[2 * WIN : 2 * WIN + 24, g * 20 : (g + 1) * 20] = gt[g * 24 : (g + 1) * 24, 256:LANES]

    table_ref[...] = tr[...].astype(bf16)
    one[WROWS:CHUNK] = jnp.zeros((CHUNK - WROWS, 128), f32)
    for i in range(SHARES):
        one[0:WROWS] = gw[i * WROWS : (i + 1) * WROWS]
        if i < 3:
            one[WROWS : WROWS + 1] = (dgain[:, :128], high, jnp.zeros((1, 128), f32))[i]
        grad_ref[i] = one[...].astype(bf16)

    hold(xt, dot(mix, wproj_ref[...], NN).astype(bf16).astype(f32))
    dhat = dnorm * gain_ref[...]
    m1 = jnp.sum(dhat, axis=1, keepdims=True) * (1.0 / C)
    m2 = jnp.sum(dhat * xhat, axis=1, keepdims=True) * (1.0 / C)
    hold(ut, rstd * (dhat - m1 - xhat * m2))
    for lev, lat, w0, w1 in window_parts():
        at = lev * 3 + lat % 3
        first = joined(get(xt, w0), get(ut, w0)).astype(bf16)
        rest = joined(get(xt, w1), get(ut, w1)).astype(bf16)
        near, far = (own_ref, lono_ref) if lat < 3 else (lato_ref, coro_ref)
        near[at * 18 : at * 18 + 12] = first
        near[at * 18 + 12 : (at + 1) * 18] = rest[0:6]
        far[at * 6 : (at + 1) * 6] = rest[6:12]


def run_main(air, up, lonh, lath, corh, gain, wqkv, wproj, bias):
    vmem = pl.BlockSpec(memory_space=pltpu.VMEM)
    tok = lambda dt: pltpu.VMEM((TOK, C), dt)
    return pl.pallas_call(
        main_kernel,
        in_specs=[vmem] * 9,
        out_specs=[vmem] * 6,
        out_shape=[
            HALOS[1],
            *HALOS,
            jax.ShapeDtypeStruct((SHARES, CHUNK, 128), bf16),
            jax.ShapeDtypeStruct((TABLE, 128), bf16),
        ],
        scratch_shapes=[
            pltpu.VMEM((2 * TOK, 128), f32),
            pltpu.VMEM((2 * TOK, 128), f32),
            pltpu.VMEM((2, WIN, HEADS * WIN), f32),
        ]
        + [tok(bf16)] * 8
        + [
            pltpu.VMEM((SHARES * WROWS, 128), f32),
            pltpu.VMEM((WIN, 384), f32),
            pltpu.VMEM((TABLE, 128), f32),
            pltpu.VMEM((CHUNK, 128), f32),
        ],
        compiler_params=pltpu.CompilerParams(vmem_limit_bytes=40 << 20),
        cost_estimate=pl.CostEstimate(flops=10**9, bytes_accessed=4 << 20, transcendentals=0),
        name="sublayer",
    )(air, up, lonh, lath, corh, gain, wqkv, wproj, bias)


def combine_kernel(air_ref, up_ref, own_ref, lonr_ref, latr_ref, corr_ref, out_ref, grad_ref):
    for lev in range(4):
        for r in range(6):
            at = lev * 3 + r % 3
            far, near = (corr_ref, latr_ref) if r < 3 else (lonr_ref, own_ref)
            far = far[at * 6 : (at + 1) * 6].astype(f32)
            near = near[at * 18 : (at + 1) * 18].astype(f32)
            rows = parted(jnp.concatenate([far, near], axis=0))
            for src, dst, row in zip((air_ref, up_ref), (out_ref, grad_ref), rows):
                dst[lev, r] = (src[lev, r].astype(f32) + row).astype(bf16)


def combine(air, up, own, lonr, latr, corr):
    vmem = pl.BlockSpec(memory_space=pltpu.VMEM)
    return pl.pallas_call(
        combine_kernel,
        in_specs=[vmem] * 6,
        out_specs=[vmem] * 2,
        out_shape=[jax.ShapeDtypeStruct(air.shape, bf16)] * 2,
        compiler_params=pltpu.CompilerParams(vmem_limit_bytes=16 << 20),
        cost_estimate=pl.CostEstimate(flops=10**10, bytes_accessed=40 << 20, transcendentals=0),
        name="combine",
    )(air, up, own, lonr, latr, corr)


def total(ref):
    parts = [ref[i].astype(f32) for i in range(ref.shape[0])]
    while len(parts) > 1:
        parts = [a + b for a, b in zip(parts[::2], parts[1::2])]
    return parts[0].astype(bf16)


def sum_kernel(*refs):
    carried = (len(refs) - 2) // 2
    parts_ref, copies_ref = refs[0], refs[1 + carried]
    one = total(parts_ref)
    for i in range(copies_ref.shape[0]):
        copies_ref[i] = one


def summed(parts, copies, *carried):
    vmem = pl.BlockSpec(memory_space=pltpu.VMEM)
    anywhere = pl.BlockSpec(memory_space=pl.ANY)
    return pl.pallas_call(
        sum_kernel,
        in_specs=[vmem] + [anywhere] * len(carried),
        out_specs=[vmem] + [anywhere] * len(carried),
        out_shape=[jax.ShapeDtypeStruct((copies, CHUNK, 128), bf16)]
        + [jax.ShapeDtypeStruct(array.shape, array.dtype) for array in carried],
        input_output_aliases={1 + i: 1 + i for i in range(len(carried))},
        compiler_params=pltpu.CompilerParams(vmem_limit_bytes=4 << 20),
        name="summed",
    )(parts, *carried)


def unpack_kernel(whole_ref, dwqkv_ref, dwproj_ref, dgain_ref, gw):
    for i in range(SHARES):
        one = whole_ref[i].astype(f32)
        gw[i * WROWS : (i + 1) * WROWS] = one[0:WROWS]
        if i == 0:
            dgain_ref[:, :128] = one[WROWS : WROWS + 1]
        if i == 1:
            dgain_ref[:, 128:] = one[WROWS : WROWS + 1, :64]
    tiles = [gw[t * C : (t + 1) * C] for t in range(6)]
    for t in range(4):
        dwqkv_ref[:, t * 128 : (t + 1) * 128] = tiles[t]
    dwqkv_ref[:, 512:576] = tiles[4][:, :64]
    dwproj_ref[...] = jnp.concatenate([tiles[4][:, 64:], tiles[5]], axis=1)


def unpack(whole):
    vmem = pl.BlockSpec(memory_space=pltpu.VMEM)
    return pl.pallas_call(
        unpack_kernel,
        in_specs=[vmem],
        out_specs=[vmem] * 3,
        out_shape=[
            jax.ShapeDtypeStruct((C, 3 * C), f32),
            jax.ShapeDtypeStruct((C, C), f32),
            jax.ShapeDtypeStruct((1, C), f32),
        ],
        scratch_shapes=[pltpu.VMEM((SHARES * WROWS, 128), f32)],
        compiler_params=pltpu.CompilerParams(vmem_limit_bytes=16 << 20),
        name="unpack",
    )(whole)


def turn_kernel(tr, dtable_ref, gt, flat):
    gt[:, 0:128] = tr[0:WIN].astype(f32)
    gt[:, 128:256] = tr[WIN : 2 * WIN].astype(f32)
    gt[:, 256:384] = jnp.zeros((WIN, 128), f32)
    last = tr[2 * WIN :].astype(f32)
    for g in range(6):
        gt[g * 24 : (g + 1) * 24, 256:LANES] = last[:24, g * 20 : (g + 1) * 20]
    lanes, rows = onehots()
    moved = dot(dot(rows, gt[...].astype(bf16), TN).astype(bf16), lanes, NT)
    for pj in range(POS):
        for pi in range(POS):
            at = (pi * POS + pj) * REL
            flat[:, at : at + REL] = moved[pj * 16 : (pj + 1) * 16, pi * REL : (pi + 1) * REL]
    for h in range(HEADS):
        dtable_ref[h] = flat[2 * h : 2 * h + 2, 0 : POS * POS * REL]


def turned(table):
    vmem = pl.BlockSpec(memory_space=pltpu.VMEM)
    return pl.pallas_call(
        turn_kernel,
        in_specs=[vmem],
        out_specs=vmem,
        out_shape=jax.ShapeDtypeStruct((HEADS, 2, POS * POS * REL), f32),
        scratch_shapes=[pltpu.VMEM((WIN, 384), f32), pltpu.VMEM((16, 3328), f32)],
        compiler_params=pltpu.CompilerParams(vmem_limit_bytes=8 << 20),
        cost_estimate=pl.CostEstimate(flops=10**9, bytes_accessed=4 << 20, transcendentals=0),
        name="turn",
    )(table)


def pairs_of(mesh_shape, lon_by, lat_by):
    lons, lats = (mesh_shape[0], mesh_shape[1])
    return [
        (i * lats + j, ((i + lon_by) % lons) * lats + (j + lat_by) % lats)
        for i in range(lons)
        for j in range(lats)
    ]


def on_device(lons, lats, air, up, gain, wqkv, wproj, table):
    def neighbour(array, lon_by, lat_by):
        if lat_by == 0:
            return lax.ppermute(array, LON, [(i, (i + lon_by) % lons) for i in range(lons)])
        if lon_by == 0:
            return lax.ppermute(array, LAT, [(i, (i + lat_by) % lats) for i in range(lats)])
        return lax.ppermute(array, LON + LAT, pairs_of((lons, lats), lon_by, lat_by))

    lonh, lath, corh = pack(air, up)
    lath = neighbour(lath, 0, -1)
    lonh = neighbour(lonh, -1, 0)
    corh = neighbour(corh, -1, -1)
    last = (lax.axis_index(LAT) == lats - 1).astype(jnp.int32).reshape(1)
    bias = prep(last, table.transpose(0, 2, 1, 3).reshape(HEADS, 2, POS * POS * REL))
    own, lono, lato, coro, grads, entries = run_main(
        air, up, lonh, lath, corh, gain.reshape(1, C), wqkv, wproj, bias
    )
    def paired(entries, step):
        other = lax.ppermute(entries, LON, [(i, i ^ step) for i in range(lons)])
        return (entries.astype(f32) + other.astype(f32)).astype(bf16)

    parts = lax.all_to_all(grads, SCATTER, split_axis=0, concat_axis=0, tiled=True)
    copies, entries, lato, lono, coro = summed(parts, 8, entries, lato, lono, coro)
    parts = lax.all_to_all(copies, REST, split_axis=0, concat_axis=0, tiled=True)
    latr = neighbour(lato, 0, 1)
    lonr = neighbour(lono, 1, 0)
    corr = neighbour(coro, 1, 1)
    for step in (1, 2, 4):
        entries = paired(entries, step)
    (copies,) = summed(parts, SHARES)
    whole = lax.all_to_all(copies, SCATTER, split_axis=0, concat_axis=0, tiled=True)
    entries = paired(entries, 8)
    d_table = turned(entries)
    block_out, d_state = combine(air, up, own, lonr, latr, corr)
    d_wqkv, d_wproj, d_gain = unpack(whole)
    d_table = d_table.reshape(1, HEADS, 2, POS * POS * REL).transpose(0, 2, 1, 3)
    return (block_out, d_state, d_gain.reshape(C), d_wqkv, d_wproj, d_table)


def solution(mesh):
    fine = Mesh(mesh.devices.reshape(4, 2, 2, 2, 4), LON + LAT)
    grid = P(None, LAT, LON, None)
    return jax.shard_map(
        functools.partial(on_device, mesh.shape["lon"], mesh.shape["lat"]),
        mesh=fine,
        in_specs=(grid, grid, P(), P(), P(), P(LAT, None, None, None)),
        out_specs=(grid, grid, P(), P(), P(), P(LAT, None, None, None)),
        check_vma=False,
    )
```

```python
import functools

import jax
import jax.numpy as jnp
from jax import lax
from jax.experimental import pallas as pl
from jax.experimental.pallas import tpu as pltpu
from jax.sharding import Mesh
from jax.sharding import PartitionSpec as P

HEADS = 6
HEAD = 32
WLEV = 2
WLAT = 6
WLON = 12
WIN = 144
POS = WLEV * WLAT
REL = 2 * WLON - 1
C = 192
TOK = 576
SHARES = 16
WROWS = 72
CHUNK = 80
TABLE = 320
LON = ("x", "yh", "core")
LAT = ("yl", "z")
SCATTER = ("yh", "yl", "z")
REST = ("x", "core")
LANES = REL * POS

epsilon = 1e-05
masked_score = -1000000000.0
f32 = jnp.float32
bf16 = jnp.bfloat16

NN = (((1,), (0,)), ((), ()))
NT = (((1,), (1,)), ((), ()))
TN = (((0,), (0,)), ((), ()))


def dot(a, b, dims):
    return lax.dot_general(a, b, dims, preferred_element_type=f32)


def window_parts():
    for a in range(2):
        for s in range(WLEV):
            for lat in range(WLAT):
                p = s * WLAT + lat
                yield (2 * a + s + 1) % 4, lat, a * 2 * WIN + p, (a * 2 + 1) * WIN + p


def put(dst, start, rows):
    n = rows.shape[0]
    dst[pl.ds(start, n, stride=POS), :] = rows[:, :128]
    high = jnp.concatenate([rows[:, 128:], jnp.zeros((n, 64), f32)], axis=1)
    dst[pl.ds(TOK + start, n, stride=POS), :] = high


def get(src, start):
    low = src[pl.ds(start, WLON, stride=POS), :]
    high = src[pl.ds(TOK + start, WLON, stride=POS), :]
    return jnp.concatenate([low, high[:, :64]], axis=1)


def whole_rows(src):
    return jnp.concatenate([src[:TOK], src[TOK : 2 * TOK][:, :64]], axis=1)


def hold(dst, rows):
    dst[:TOK] = rows[:, :128]
    dst[TOK : 2 * TOK, :64] = rows[:, 128:]


def joined(state, up):
    return jnp.concatenate([state[:, :128], up[:, :128], state[:, 128:], up[:, 128:]], axis=1)


def parted(rows):
    state = jnp.concatenate([rows[:, 0:128], rows[:, 256:320]], axis=1)
    return state, jnp.concatenate([rows[:, 128:256], rows[:, 320:384]], axis=1)


def pack_kernel(air_hbm, up_hbm, lonh_ref, lath_ref, corh_ref, low, high, sems):
    copies = []
    for i, src in enumerate((air_hbm, up_hbm)):
        for lev in range(4):
            copies.append(
                pltpu.make_async_copy(src.at[lev, 0:3], low.at[i, lev], sems.at[0, i, lev])
            )
            copies.append(
                pltpu.make_async_copy(
                    src.at[lev, 3:6, 0:8], high.at[i, lev], sems.at[1, i, lev]
                )
            )
    for copy in copies:
        copy.start()
    for copy in copies:
        copy.wait()
    for lev in range(4):
        for r in range(3):
            at = lev * 3 + r
            row = joined(low[0, lev, r].astype(f32), low[1, lev, r].astype(f32)).astype(bf16)
            corh_ref[at * 6 : (at + 1) * 6] = row[0:6]
            lath_ref[at * 18 : (at + 1) * 18] = row[6:24]
            row = joined(high[0, lev, r].astype(f32), high[1, lev, r].astype(f32))
            lonh_ref[at * 6 : (at + 1) * 6] = row.astype(bf16)[0:6]


HALOS = [
    jax.ShapeDtypeStruct((80, 2 * C), bf16),
    jax.ShapeDtypeStruct((224, 2 * C), bf16),
    jax.ShapeDtypeStruct((80, 2 * C), bf16),
]


def pack(air, up):
    vmem = pl.BlockSpec(memory_space=pltpu.VMEM)
    hbm = pl.BlockSpec(memory_space=pltpu.HBM)
    return pl.pallas_call(
        pack_kernel,
        in_specs=[hbm] * 2,
        out_specs=[vmem] * 3,
        out_shape=HALOS,
        scratch_shapes=[
            pltpu.VMEM((2, 4, 3, 24, C), bf16),
            pltpu.VMEM((2, 4, 3, 8, C), bf16),
            pltpu.SemaphoreType.DMA((2, 2, 4)),
        ],
        compiler_params=pltpu.CompilerParams(vmem_limit_bytes=8 << 20),
        name="pack",
    )(
        pltpu.with_memory_space_constraint(air, pltpu.HBM),
        pltpu.with_memory_space_constraint(up, pltpu.HBM),
    )


def normalised(x):
    mean = jnp.sum(x, axis=1, keepdims=True) * (1.0 / C)
    centred = x - mean
    var = jnp.sum(centred * centred, axis=1, keepdims=True) * (1.0 / C)
    rstd = lax.rsqrt(var + epsilon)
    return centred * rstd, rstd


def onehots():
    src = lax.broadcasted_iota(jnp.int32, (384, 384), 0)
    dst = lax.broadcasted_iota(jnp.int32, (384, 384), 1)
    wanted = (dst % POS) * REL + (REL - 1 - dst // POS)
    lanes = ((src == wanted) & (dst < LANES)).astype(f32).astype(bf16)
    to = lax.broadcasted_iota(jnp.int32, (WIN, 192), 0)
    at = lax.broadcasted_iota(jnp.int32, (WIN, 192), 1)
    ah = to // POS
    rows = (at == (to % POS) * 16 + (ah % HEADS) * 2 + ah // HEADS).astype(f32).astype(bf16)
    return lanes, rows


def prep_kernel(last_ref, table_ref, bias, apart, held):
    entries = jnp.concatenate([table_ref[h] for h in range(HEADS)], axis=0)
    apart[...] = jnp.zeros_like(apart)
    for pj in range(POS):
        for pi in range(POS):
            at = (pi * POS + pj) * REL
            apart[pj * 16 : pj * 16 + POS, pi * REL : (pi + 1) * REL] = entries[:, at : at + REL]
    lanes, rows = onehots()
    left = apart[...]
    total = None
    for _ in range(3):
        piece = left.astype(bf16)
        left = left - piece.astype(f32)
        moved = dot(rows, dot(piece, lanes, NN).astype(bf16), NN)
        total = moved if total is None else total + moved
    held[...] = total
    for a in range(2):
        for h in range(HEADS):
            at = (a * HEADS + h) * POS
            for lon in range(WLON):
                bias[a, lon * POS : (lon + 1) * POS, h * WIN : (h + 1) * WIN] = held[
                    at : at + POS, (11 - lon) * POS : (11 - lon) * POS + WIN
                ]
    is_last = last_ref[0]
    for a in range(2):
        pj = lax.broadcasted_iota(jnp.int32, (WIN, 1), 0) % POS
        pi = lax.broadcasted_iota(jnp.int32, (1, HEADS * WIN), 1) % POS

        def region(p):
            lev_part = jnp.where(p >= WLAT, 2 * a, 0)
            lat_part = jnp.where((p % WLAT) >= WLAT // 2, is_last, 0)
            return lev_part + lat_part

        bias[a] = jnp.where(region(pj) == region(pi), bias[a], masked_score)


def prep(last, table):
    vmem = pl.BlockSpec(memory_space=pltpu.VMEM)
    smem = pl.BlockSpec(memory_space=pltpu.SMEM)
    return pl.pallas_call(
        prep_kernel,
        in_specs=[smem, vmem],
        out_specs=vmem,
        out_shape=jax.ShapeDtypeStruct((2, WIN, HEADS * WIN), f32),
        scratch_shapes=[pltpu.VMEM((192, 384), f32), pltpu.VMEM((WIN, 384), f32)],
        compiler_params=pltpu.CompilerParams(vmem_limit_bytes=16 << 20),
        cost_estimate=pl.CostEstimate(flops=10**8, bytes_accessed=2 << 20, transcendentals=0),
        name="prep",
    )(last, table)


def main_kernel(
    air_ref, up_ref, lonh_ref, lath_ref, corh_ref, gain_ref, wqkv_ref, wproj_ref, bias,
    own_ref, lono_ref, lato_ref, coro_ref, grad_ref, table_ref,
    xt, ut, dbias, q_s, k_s, v_s, dm_s, mix_s, dq_s, dk_s, dv_s, gw, gt, tr, one,
):
    for lev, lat, w0, w1 in window_parts():
        at = lev * 3 + lat % 3
        if lat < 3:
            rows = [src[lev, lat + 3].astype(f32) for src in (air_ref, up_ref)]
            far = parted(lonh_ref[at * 6 : (at + 1) * 6].astype(f32))
            shift = 6
        else:
            rows = parted(lath_ref[at * 18 : (at + 1) * 18].astype(f32))
            far = parted(corh_ref[at * 6 : (at + 1) * 6].astype(f32))
            shift = 0
        for dst, row, edge in zip((xt, ut), rows, far):
            put(dst, w0, row[shift : shift + 12])
            put(dst, w1, row[shift + 12 : shift + 18])
            put(dst, w1 + 72, edge)

    dbias[...] = jnp.zeros_like(dbias)

    x = whole_rows(xt)
    xhat, rstd = normalised(x)
    normed = (xhat * gain_ref[...]).astype(bf16)
    for part, dst in enumerate((q_s, k_s, v_s)):
        dst[...] = dot(normed, wqkv_ref[:, part * C : (part + 1) * C], NN).astype(bf16)
    up = whole_rows(ut).astype(bf16)
    dm_s[...] = dot(up, wproj_ref[...], NT).astype(bf16)

    scale = HEAD**-0.5
    lane_head = lax.broadcasted_iota(jnp.int32, (1, C), 1) // HEAD

    def spread(rows):
        zero = jnp.zeros_like(rows)
        return jnp.concatenate([jnp.where(lane_head == h, rows, zero) for h in range(HEADS)], axis=0)

    def gathered(stacked):
        total = stacked[0:WIN]
        for h in range(1, HEADS):
            total = jnp.where(lane_head == h, stacked[h * WIN : (h + 1) * WIN], total)
        return total

    def begin(w):
        rows = pl.ds(w * WIN, WIN)
        qs = spread(q_s[rows, :])
        scores = dot(k_s[rows, :], qs, NT)
        return rows, qs, scores, dot(v_s[rows, :], spread(dm_s[rows, :]), NT)

    def middle(w, state):
        rows, qs, scores, dprobs = state
        a = w // 2
        scores = scores * scale + bias[a]
        top = jnp.max(scores, axis=0, keepdims=True)
        weights = jnp.exp(scores - top)
        probs = weights * (1.0 / jnp.sum(weights, axis=0, keepdims=True))
        inner = jnp.sum(probs * dprobs, axis=0, keepdims=True)
        dscores = probs * (dprobs - inner)
        dbias[a] += dscores
        return rows, qs, probs.astype(bf16), dscores.astype(bf16)

    def end(w, state):
        rows, qs, soft, dsc = state
        mix_s[rows, :] = gathered(dot(soft, v_s[rows, :], TN)).astype(bf16)
        dv_s[rows, :] = dot(soft, spread(dm_s[rows, :]), NN).astype(bf16)
        dk_s[rows, :] = (dot(dsc, qs, NN) * scale).astype(bf16)
        dq_s[rows, :] = (gathered(dot(dsc, k_s[rows, :], TN)) * scale).astype(bf16)

    ready = begin(0)
    for w in range(4):
        done = middle(w, ready)
        if w < 3:
            ready = begin(w + 1)
        end(w, done)

    mix = mix_s[...]
    mq, mk, mv = (dot(normed, d[...], TN) for d in (dq_s, dk_s, dv_s))
    mp = dot(mix, up, TN)
    wide = lambda m, n: jnp.concatenate([m[:, 128:], n[:, :64]], axis=1)
    tiles = (mq[:, :128], wide(mq, mk), mk[:, 64:], mv[:, :128], wide(mv, mp), mp[:, 64:])
    for t, m in enumerate(tiles):
        gw[t * C : (t + 1) * C, :] = m
    dnorm = (
        dot(dq_s[...], wqkv_ref[:, 0:C], NT)
        + dot(dk_s[...], wqkv_ref[:, C : 2 * C], NT)
        + dot(dv_s[...], wqkv_ref[:, 2 * C : 3 * C], NT)
    )
    dgain = jnp.sum(dnorm * xhat, axis=0, keepdims=True)
    high = jnp.concatenate([dgain[:, 128:192], jnp.zeros((1, 64), f32)], axis=1)

    gt[...] = jnp.zeros_like(gt)
    for a in range(2):
        for h in range(HEADS):
            rows = pl.ds((a * HEADS + h) * POS, POS)
            for lon in range(WLON):
                gt[rows, (11 - lon) * POS : (11 - lon) * POS + WIN] += dbias[
                    a, lon * POS : (lon + 1) * POS, h * WIN : (h + 1) * WIN
                ]
    tr[0:WIN] = gt[:, 0:128]
    tr[WIN : 2 * WIN] = gt[:, 128:256]
    tr[2 * WIN :] = jnp.zeros((TABLE - 2 * WIN, 128), f32)
    for g in range(6):
        tr[2 * WIN : 2 * WIN + 24, g * 20 : (g + 1) * 20] = gt[g * 24 : (g + 1) * 24, 256:LANES]

    table_ref[...] = tr[...].astype(bf16)
    one[WROWS:CHUNK] = jnp.zeros((CHUNK - WROWS, 128), f32)
    for i in range(SHARES):
        one[0:WROWS] = gw[i * WROWS : (i + 1) * WROWS]
        if i < 3:
            one[WROWS : WROWS + 1] = (dgain[:, :128], high, jnp.zeros((1, 128), f32))[i]
        grad_ref[i] = one[...].astype(bf16)

    hold(xt, dot(mix, wproj_ref[...], NN).astype(bf16).astype(f32))
    dhat = dnorm * gain_ref[...]
    m1 = jnp.sum(dhat, axis=1, keepdims=True) * (1.0 / C)
    m2 = jnp.sum(dhat * xhat, axis=1, keepdims=True) * (1.0 / C)
    hold(ut, rstd * (dhat - m1 - xhat * m2))
    for lev, lat, w0, w1 in window_parts():
        at = lev * 3 + lat % 3
        first = joined(get(xt, w0), get(ut, w0)).astype(bf16)
        rest = joined(get(xt, w1), get(ut, w1)).astype(bf16)
        near, far = (own_ref, lono_ref) if lat < 3 else (lato_ref, coro_ref)
        near[at * 18 : at * 18 + 12] = first
        near[at * 18 + 12 : (at + 1) * 18] = rest[0:6]
        far[at * 6 : (at + 1) * 6] = rest[6:12]


def run_main(air, up, lonh, lath, corh, gain, wqkv, wproj, bias):
    vmem = pl.BlockSpec(memory_space=pltpu.VMEM)
    tok = lambda dt: pltpu.VMEM((TOK, C), dt)
    return pl.pallas_call(
        main_kernel,
        in_specs=[vmem] * 9,
        out_specs=[vmem] * 6,
        out_shape=[
            HALOS[1],
            *HALOS,
            jax.ShapeDtypeStruct((SHARES, CHUNK, 128), bf16),
            jax.ShapeDtypeStruct((TABLE, 128), bf16),
        ],
        scratch_shapes=[
            pltpu.VMEM((2 * TOK + 128, 128), f32),
            pltpu.VMEM((2 * TOK + 128, 128), f32),
            pltpu.VMEM((2, WIN, HEADS * WIN), f32),
        ]
        + [tok(bf16)] * 8
        + [
            pltpu.VMEM((SHARES * WROWS, 128), f32),
            pltpu.VMEM((WIN, 384), f32),
            pltpu.VMEM((TABLE, 128), f32),
            pltpu.VMEM((CHUNK, 128), f32),
        ],
        compiler_params=pltpu.CompilerParams(vmem_limit_bytes=40 << 20),
        cost_estimate=pl.CostEstimate(flops=10**9, bytes_accessed=4 << 20, transcendentals=0),
        name="sublayer",
    )(air, up, lonh, lath, corh, gain, wqkv, wproj, bias)


def combine_kernel(air_ref, up_ref, own_ref, lonr_ref, latr_ref, corr_ref, out_ref, grad_ref):
    for lev in range(4):
        for r in range(6):
            at = lev * 3 + r % 3
            far, near = (corr_ref, latr_ref) if r < 3 else (lonr_ref, own_ref)
            far = far[at * 6 : (at + 1) * 6].astype(f32)
            near = near[at * 18 : (at + 1) * 18].astype(f32)
            rows = parted(jnp.concatenate([far, near], axis=0))
            for src, dst, row in zip((air_ref, up_ref), (out_ref, grad_ref), rows):
                dst[lev, r] = (src[lev, r].astype(f32) + row).astype(bf16)


def combine(air, up, own, lonr, latr, corr):
    vmem = pl.BlockSpec(memory_space=pltpu.VMEM)
    return pl.pallas_call(
        combine_kernel,
        in_specs=[vmem] * 6,
        out_specs=[vmem] * 2,
        out_shape=[jax.ShapeDtypeStruct(air.shape, bf16)] * 2,
        compiler_params=pltpu.CompilerParams(vmem_limit_bytes=16 << 20),
        cost_estimate=pl.CostEstimate(flops=10**10, bytes_accessed=40 << 20, transcendentals=0),
        name="combine",
    )(air, up, own, lonr, latr, corr)


def total(ref):
    parts = [ref[i].astype(f32) for i in range(ref.shape[0])]
    while len(parts) > 1:
        parts = [a + b for a, b in zip(parts[::2], parts[1::2])]
    return parts[0].astype(bf16)


def sum_kernel(*refs):
    carried = (len(refs) - 2) // 2
    parts_ref, copies_ref = refs[0], refs[1 + carried]
    one = total(parts_ref)
    for i in range(copies_ref.shape[0]):
        copies_ref[i] = one


def summed(parts, copies, *carried):
    vmem = pl.BlockSpec(memory_space=pltpu.VMEM)
    anywhere = pl.BlockSpec(memory_space=pl.ANY)
    return pl.pallas_call(
        sum_kernel,
        in_specs=[vmem] + [anywhere] * len(carried),
        out_specs=[vmem] + [anywhere] * len(carried),
        out_shape=[jax.ShapeDtypeStruct((copies, CHUNK, 128), bf16)]
        + [jax.ShapeDtypeStruct(array.shape, array.dtype) for array in carried],
        input_output_aliases={1 + i: 1 + i for i in range(len(carried))},
        compiler_params=pltpu.CompilerParams(vmem_limit_bytes=4 << 20),
        name="summed",
    )(parts, *carried)


def unpack_kernel(whole_ref, dwqkv_ref, dwproj_ref, dgain_ref, gw):
    for i in range(SHARES):
        one = whole_ref[i].astype(f32)
        gw[i * WROWS : (i + 1) * WROWS] = one[0:WROWS]
        if i == 0:
            dgain_ref[:, :128] = one[WROWS : WROWS + 1]
        if i == 1:
            dgain_ref[:, 128:] = one[WROWS : WROWS + 1, :64]
    tiles = [gw[t * C : (t + 1) * C] for t in range(6)]
    for t in range(4):
        dwqkv_ref[:, t * 128 : (t + 1) * 128] = tiles[t]
    dwqkv_ref[:, 512:576] = tiles[4][:, :64]
    dwproj_ref[...] = jnp.concatenate([tiles[4][:, 64:], tiles[5]], axis=1)


def unpack(whole):
    vmem = pl.BlockSpec(memory_space=pltpu.VMEM)
    return pl.pallas_call(
        unpack_kernel,
        in_specs=[vmem],
        out_specs=[vmem] * 3,
        out_shape=[
            jax.ShapeDtypeStruct((C, 3 * C), f32),
            jax.ShapeDtypeStruct((C, C), f32),
            jax.ShapeDtypeStruct((1, C), f32),
        ],
        scratch_shapes=[pltpu.VMEM((SHARES * WROWS, 128), f32)],
        compiler_params=pltpu.CompilerParams(vmem_limit_bytes=16 << 20),
        name="unpack",
    )(whole)


def turn_kernel(tr, dtable_ref, gt, flat):
    gt[:, 0:128] = tr[0:WIN].astype(f32)
    gt[:, 128:256] = tr[WIN : 2 * WIN].astype(f32)
    gt[:, 256:384] = jnp.zeros((WIN, 128), f32)
    last = tr[2 * WIN :].astype(f32)
    for g in range(6):
        gt[g * 24 : (g + 1) * 24, 256:LANES] = last[:24, g * 20 : (g + 1) * 20]
    lanes, rows = onehots()
    moved = dot(dot(rows, gt[...].astype(bf16), TN).astype(bf16), lanes, NT)
    for pj in range(POS):
        for pi in range(POS):
            at = (pi * POS + pj) * REL
            flat[:, at : at + REL] = moved[pj * 16 : (pj + 1) * 16, pi * REL : (pi + 1) * REL]
    for h in range(HEADS):
        dtable_ref[h] = flat[2 * h : 2 * h + 2, 0 : POS * POS * REL]


def turned(table):
    vmem = pl.BlockSpec(memory_space=pltpu.VMEM)
    return pl.pallas_call(
        turn_kernel,
        in_specs=[vmem],
        out_specs=vmem,
        out_shape=jax.ShapeDtypeStruct((HEADS, 2, POS * POS * REL), f32),
        scratch_shapes=[pltpu.VMEM((WIN, 384), f32), pltpu.VMEM((16, 3328), f32)],
        compiler_params=pltpu.CompilerParams(vmem_limit_bytes=8 << 20),
        cost_estimate=pl.CostEstimate(flops=10**9, bytes_accessed=4 << 20, transcendentals=0),
        name="turn",
    )(table)


def pairs_of(mesh_shape, lon_by, lat_by):
    lons, lats = (mesh_shape[0], mesh_shape[1])
    return [
        (i * lats + j, ((i + lon_by) % lons) * lats + (j + lat_by) % lats)
        for i in range(lons)
        for j in range(lats)
    ]


def on_device(lons, lats, air, up, gain, wqkv, wproj, table):
    def neighbour(array, lon_by, lat_by):
        if lat_by == 0:
            return lax.ppermute(array, LON, [(i, (i + lon_by) % lons) for i in range(lons)])
        if lon_by == 0:
            return lax.ppermute(array, LAT, [(i, (i + lat_by) % lats) for i in range(lats)])
        return lax.ppermute(array, LON + LAT, pairs_of((lons, lats), lon_by, lat_by))

    lonh, lath, corh = pack(air, up)
    lath = neighbour(lath, 0, -1)
    lonh = neighbour(lonh, -1, 0)
    corh = neighbour(corh, -1, -1)
    last = (lax.axis_index(LAT) == lats - 1).astype(jnp.int32).reshape(1)
    bias = prep(last, table.transpose(0, 2, 1, 3).reshape(HEADS, 2, POS * POS * REL))
    own, lono, lato, coro, grads, entries = run_main(
        air, up, lonh, lath, corh, gain.reshape(1, C), wqkv, wproj, bias
    )
    def paired(entries, step):
        other = lax.ppermute(entries, LON, [(i, i ^ step) for i in range(lons)])
        return (entries.astype(f32) + other.astype(f32)).astype(bf16)

    parts = lax.all_to_all(grads, SCATTER, split_axis=0, concat_axis=0, tiled=True)
    copies, entries, lato, lono, coro = summed(parts, 8, entries, lato, lono, coro)
    parts = lax.all_to_all(copies, REST, split_axis=0, concat_axis=0, tiled=True)
    latr = neighbour(lato, 0, 1)
    lonr = neighbour(lono, 1, 0)
    corr = neighbour(coro, 1, 1)
    for step in (1, 2, 4):
        entries = paired(entries, step)
    (copies,) = summed(parts, SHARES)
    whole = lax.all_to_all(copies, SCATTER, split_axis=0, concat_axis=0, tiled=True)
    entries = paired(entries, 8)
    d_table = turned(entries)
    block_out, d_state = combine(air, up, own, lonr, latr, corr)
    d_wqkv, d_wproj, d_gain = unpack(whole)
    d_table = d_table.reshape(1, HEADS, 2, POS * POS * REL).transpose(0, 2, 1, 3)
    return (block_out, d_state, d_gain.reshape(C), d_wqkv, d_wproj, d_table)


def solution(mesh):
    fine = Mesh(mesh.devices.reshape(4, 2, 2, 2, 4), LON + LAT)
    grid = P(None, LAT, LON, None)
    return jax.shard_map(
        functools.partial(on_device, mesh.shape["lon"], mesh.shape["lat"]),
        mesh=fine,
        in_specs=(grid, grid, P(), P(), P(), P(LAT, None, None, None)),
        out_specs=(grid, grid, P(), P(), P(), P(LAT, None, None, None)),
        check_vma=False,
    )
```
